256 devices in a mesh: ctx: 32 (over x, y, core), tp: 8 (over z).
Axes of the slice: x: 4, y: 4, z: 8, core: 2. Of those that a mesh axis runs over, the one named last changes fastest.
Arguments:
- upstream: bfloat16 [32768, 4096], P('ctx', 'tp'), may hold values from -0.75 to 0.75
- out_weight: bfloat16 [4096, 4096], P('tp'), may hold values from -0.125 to 0.125
- inner_act: bfloat16 [32768, 4096], P('ctx', 'tp'), may hold values from -6 to 6
- head_bc: bfloat16 [32768, 4096], P('ctx', 'tp'), may hold values from -0.75 to 0.75
- log_decay: float32 [32, 32768], P('tp', 'ctx'), may hold values from -1 to 0, as said below
- states: float32 [128, 32, 64, 128], P('ctx', 'tp'), may hold values from -3 to 3
- skip: float32 [32], P('tp'), may hold values from 0.1 to 1.9
Outputs:
- grad_inner: bfloat16 [32768, 4096], P('ctx', 'tp')
- grad_bc: float32 [32768, 4096], P('ctx', 'tp')
- grad_log: float32 [32, 32768], P('tp', 'ctx')
The draws below stay inside these ranges and needn't reach their ends.
Inputs may be any that keep to these rules, and one draw needn't show every extreme that they name: `log_decay`: every entry is negative.
All inputs are finite; a program needn't handle non-finite values.
Results may differ from the reference program's by a relative error of at most 0.0049.
Values may be sent and summed in bfloat16 or wider, within the bound.
No kernel may reach another device: no remote copies, remote signals or barrier semaphores. Data moves between devices by JAX's collectives and lax.ppermute only.
A program may use at most 128 MiB of HBM per device.

```python
import math
import jax
import jax.numpy as jnp
from jax import lax

D = 4096
HEAD_TOTAL = 32
HEAD_DIM = 128
STATE = 64
BLOCK = 256
TOK_DEV = 1024
INNER = 4096
SEQUENCE_LENGTH = 32768
BLOCKS = 128


def draw_log_decay(key, part):
    random_keys = jax.random.split(jax.random.fold_in(key, 17), 7)
    fast_cut = 4
    fast = jax.random.randint(random_keys[0], (HEAD_TOTAL,), 0, 8) < fast_cut
    fast_rate = jax.random.uniform(random_keys[1], (HEAD_TOTAL,), jnp.float32, 1.0 / 50.0, 1.0 / 30.0)
    slow_rate = jax.random.uniform(random_keys[2], (HEAD_TOTAL,), jnp.float32, 0.02, 0.1) / SEQUENCE_LENGTH
    decay_rate = jnp.where(fast, fast_rate, slow_rate)
    rough_estimate = jnp.exp(jax.random.uniform(random_keys[3], (HEAD_TOTAL, SEQUENCE_LENGTH), jnp.float32, -math.log(2.0), math.log(2.0)))
    partition_scale = jnp.exp(jax.random.uniform(random_keys[4], (HEAD_TOTAL, SEQUENCE_LENGTH // TOK_DEV), jnp.float32, -math.log(2.0), math.log(2.0)))
    partition_scale = jnp.repeat(partition_scale, TOK_DEV, axis=1)
    spots = jax.random.randint(random_keys[5], (HEAD_TOTAL, 3), 0, SEQUENCE_LENGTH)
    places = jnp.arange(SEQUENCE_LENGTH, dtype=jnp.int32)
    masked_scores = jnp.any(places[None, None, :] == spots[:, :, None], axis=1)
    decay_products = jax.random.uniform(random_keys[6], (HEAD_TOTAL, SEQUENCE_LENGTH), jnp.float32, 0.223, 0.693)
    return -(decay_rate[:, None] * rough_estimate * partition_scale + jnp.where(masked_scores, decay_products, 0.0))


def with_spikes(result, key, source, target, parts, factor):
    owner, partner = [(jnp.arange(result.shape[position]) // (result.shape[position] // parts)).reshape([-1 if axis == position else 1 for axis in range(result.ndim)]) for position in (source, target)]
    chosen = jax.random.permutation(key, parts)[partner]
    strong = (owner == chosen) | (owner == (partner + parts // 2) % parts)
    return jnp.where(strong, factor * result, result)


def block_levels(own_key, extent, cuts, smallest, top_value):
    loudness = 1.0
    for dim, shards_of in cuts:
        heights = jax.random.uniform(jax.random.fold_in(jax.random.fold_in(own_key, 6), dim), (shards_of,), jnp.float32, smallest / len(cuts), top_value / len(cuts))
        loudness = loudness * jnp.repeat(jnp.exp(heights), extent[dim] // shards_of).reshape((-1,) + (1,) * (len(extent) - 1 - dim))
    return loudness


def centred(stream_key, shape, deviation, bound, cuts=(), held_as=jnp.bfloat16):
    drawn = deviation * jax.random.normal(stream_key, shape, jnp.float32)
    if cuts:
        drawn = drawn * block_levels(stream_key, shape, cuts, -0.22, 0.18)
    return jnp.clip(drawn, -bound, bound).astype(held_as)


def noise_with(stream_key, extent, width, bound, cuts, heavy, held_as=jnp.bfloat16):
    values = width * jax.random.normal(stream_key, extent, jnp.float32)
    if cuts:
        values = values * block_levels(stream_key, extent, cuts, -0.22, 0.18)
    return jnp.clip(with_spikes(values, jax.random.fold_in(stream_key, 3), *heavy), -bound, bound).astype(held_as)


def setup_inputs(seed: int = 0) -> dict:
    streams_of = jax.random.split(jax.random.key(seed), 8)
    upstream = centred(streams_of[0], (SEQUENCE_LENGTH, D), 0.125, 0.75, ((0, 32), (1, 8)))
    out_weight = noise_with(streams_of[1], (INNER, D), D ** -0.5, 0.125, ((0, 8),), (1, 0, 8, 2.0))
    inner_act = centred(streams_of[2], (SEQUENCE_LENGTH, INNER), 1.0, 6.0, ((0, 32), (1, 8)))
    head_bc = centred(streams_of[3], (SEQUENCE_LENGTH, HEAD_TOTAL * 2 * STATE), 0.125, 0.75, ((0, 32), (1, 8)))
    log_decay = draw_log_decay(jax.random.fold_in(streams_of[7], 71), 0)
    states = centred(streams_of[5], (BLOCKS, HEAD_TOTAL, STATE, HEAD_DIM), 0.5, 3.0, ((0, 32), (1, 8)), jnp.float32)
    skip = jnp.clip(1.0 + 0.18 * jax.random.normal(streams_of[6], (HEAD_TOTAL,), jnp.float32), 0.1, 1.9)
    return dict(upstream=upstream, out_weight=out_weight, inner_act=inner_act, head_bc=head_bc, log_decay=log_decay, states=states, skip=skip)


def state_end(values, b_rows, log_rate, start_state):
    cumlog = jnp.cumsum(log_rate)
    tail_decay = jnp.exp(cumlog[-1] - cumlog)
    weighted = b_rows * tail_decay[:, None]
    return jnp.exp(cumlog[-1]) * start_state + jnp.dot(weighted.T, values, precision=lax.Precision.HIGHEST)

def block_forward(values, b_rows, c_rows, log_rate, start_state):
    cumlog = jnp.cumsum(log_rate)
    log_gap = cumlog[:, None] - cumlog[None, :]
    row_ids = lax.broadcasted_iota(jnp.int32, log_gap.shape, 0)
    col_ids = lax.broadcasted_iota(jnp.int32, log_gap.shape, 1)
    decays = jnp.where(row_ids >= col_ids, jnp.exp(jnp.minimum(log_gap, 0.0)), 0.0)
    scores = jnp.dot(c_rows, b_rows.T, precision=lax.Precision.HIGHEST) * decays
    output = jnp.dot(scores, values, precision=lax.Precision.HIGHEST)
    output = output + jnp.exp(cumlog)[:, None] * jnp.dot(c_rows, start_state, precision=lax.Precision.HIGHEST)
    return (output, state_end(values, b_rows, log_rate, start_state))

def block_gradient_pass(values, b_rows, c_rows, log_rate, start_state, out_grad, carried_state):
    unused, pullback = jax.vjp(block_forward, values, b_rows, c_rows, log_rate, start_state)
    return pullback((out_grad, carried_state))

def reference(upstream, out_weight, inner_act, head_bc, log_decay, states, skip):
    out_grad = jnp.dot(upstream, out_weight.T, preferred_element_type=jnp.float32).astype(jnp.bfloat16)
    grad_vals = out_grad.astype(jnp.float32).reshape(BLOCKS, BLOCK, HEAD_TOTAL, HEAD_DIM).transpose(2, 0, 1, 3)
    inner_vals = inner_act.astype(jnp.float32).reshape(BLOCKS, BLOCK, HEAD_TOTAL, HEAD_DIM).transpose(2, 0, 1, 3)
    bc_vals = head_bc.astype(jnp.float32).reshape(BLOCKS, BLOCK, HEAD_TOTAL, 2, STATE).transpose(2, 0, 1, 3, 4)
    b_vals = bc_vals[:, :, :, 0, :]
    c_vals = bc_vals[:, :, :, 1, :]
    log_vals = log_decay.reshape(HEAD_TOTAL, BLOCKS, BLOCK)
    start_vals = states.transpose(1, 0, 2, 3)

    def head_grads(items):
        values, b_head, c_head, log_rate, start_state, head_grad = items

        def step(carried_state, block_entries):
            input_value, input_proj_value, output_proj_value, log_decay_value, state_value, output_gradient_value = block_entries
            input_gradient, input_proj_gradient, output_proj_gradient, log_decay_gradient, state_gradient = block_gradient_pass(input_value, input_proj_value, output_proj_value, log_decay_value, state_value, output_gradient_value, carried_state)
            return (state_gradient, (input_gradient, input_proj_gradient, output_proj_gradient, log_decay_gradient))
        start = jnp.zeros((STATE, HEAD_DIM), jnp.float32)
        unused, outputs = lax.scan(step, start, (values, b_head, c_head, log_rate, start_state, head_grad), reverse=True)
        return outputs
    input_gradient, input_proj_gradient, output_proj_gradient, log_decay_gradient = lax.map(head_grads, (inner_vals, b_vals, c_vals, log_vals, start_vals, grad_vals))
    input_gradient = input_gradient + skip[:, None, None, None] * grad_vals
    grad_inner = input_gradient.transpose(1, 2, 0, 3).reshape(SEQUENCE_LENGTH, INNER).astype(jnp.bfloat16)
    grad_pair = jnp.stack([input_proj_gradient, output_proj_gradient], axis=3)
    grad_bc = grad_pair.transpose(1, 2, 0, 3, 4).reshape(SEQUENCE_LENGTH, HEAD_TOTAL * 2 * STATE)
    grad_log = log_decay_gradient.reshape(HEAD_TOTAL, SEQUENCE_LENGTH)
    return (grad_inner, grad_bc, grad_log)
```

```python
import jax
import jax.numpy as jnp
from jax import lax
from jax.experimental import pallas as pl
from jax.experimental.pallas import tpu as pltpu
from jax.sharding import PartitionSpec as P

HEAD_DIM = 128
STATE = 64
BLOCK = 256
F32 = jnp.float32
BF16 = jnp.bfloat16
VMEM_LIMIT = 48 << 20


def dot(a, b, dims):
    return lax.dot_general(a, b, (dims, ((), ())), preferred_element_type=F32)


NN = ((1,), (0,))
NT = ((1,), (1,))
TN = ((0,), (0,))


def low_lanes(shape):
    return lax.broadcasted_iota(jnp.int32, shape, len(shape) - 1) < STATE


def prepare_kernel(heads, a_last, bc_ref, sw_ref, arow_ref, acol_ref, dec_ref, sct_ref, wct_ref, wb_ref):
    b = pl.program_id(0)
    rows = lax.broadcasted_iota(jnp.int32, (BLOCK, BLOCK), 0)
    cols = lax.broadcasted_iota(jnp.int32, (BLOCK, BLOCK), 1)
    low = low_lanes((BLOCK, HEAD_DIM))
    for h in range(heads):
        lanes = slice(h * HEAD_DIM, (h + 1) * HEAD_DIM)
        row = arow_ref[h : h + 1, :]
        col1 = acol_ref[:, lanes]
        col = jnp.concatenate([col1, col1], axis=1)
        gap = col - row
        dec_ref[0, h] = jnp.where(rows >= cols, jnp.exp(jnp.minimum(gap, 0.0)), 0.0).astype(BF16)
        bc = bc_ref[:, lanes]
        sw = sw_ref[:, lanes]
        zero = jnp.zeros_like(bc)
        c_low = jnp.where(low, sw, zero)
        b_low = jnp.where(low, bc, zero)
        scores = dot(b_low, c_low, NT)
        back = jnp.where(cols >= rows, jnp.exp(jnp.minimum(-gap, 0.0)), 0.0)
        sct_ref[0, h] = (scores * back).astype(BF16)
        weighted = c_low.astype(F32) * jnp.exp(col1)
        wct_ref[0, h] = weighted.T[:STATE, :].astype(BF16)
        tail = jnp.exp(a_last[b, h] - col1)
        wb_ref[:, lanes] = (b_low.astype(F32) * tail).astype(BF16)


def prepare_body(heads):
    def body(a_last, bc_ref, sw_ref, arow_ref, acol_ref, dec_ref, sct_ref, wct_ref, wb_ref):
        prepare_kernel(heads, a_last, bc_ref, sw_ref, arow_ref, acol_ref, dec_ref, sct_ref, wct_ref, wb_ref)

    return body


def prepare(a_last, bc, sw, arow, acol):
    tokens, width = bc.shape
    heads = width // HEAD_DIM
    blocks = tokens // BLOCK
    wide = pl.BlockSpec((BLOCK, width), lambda b: (b, 0))
    square = pl.BlockSpec((1, heads, BLOCK, BLOCK), lambda b: (b, 0, 0, 0))
    return pl.pallas_call(
        prepare_body(heads),
        name="prepare",
        grid=(blocks,),
        in_specs=[
            pl.BlockSpec(memory_space=pltpu.SMEM),
            wide,
            wide,
            pl.BlockSpec((heads, BLOCK), lambda b: (0, b)),
            wide,
        ],
        out_specs=[
            square,
            square,
            pl.BlockSpec((1, heads, STATE, BLOCK), lambda b: (b, 0, 0, 0)),
            wide,
        ],
        out_shape=[
            jax.ShapeDtypeStruct((blocks, heads, BLOCK, BLOCK), BF16),
            jax.ShapeDtypeStruct((blocks, heads, BLOCK, BLOCK), BF16),
            jax.ShapeDtypeStruct((blocks, heads, STATE, BLOCK), BF16),
            jax.ShapeDtypeStruct((tokens, width), BF16),
        ],
        cost_estimate=pl.CostEstimate(flops=4_000_000_000, bytes_accessed=9_000_000, transcendentals=0),
        compiler_params=pltpu.CompilerParams(vmem_limit_bytes=VMEM_LIMIT),
    )(a_last, bc, sw, arow, acol)


def close_chunk(first, acc, up, down, weight, wct, scale, earlier):
    tokens, width = acc.shape
    heads = width // HEAD_DIM
    last = earlier is not None

    def body(*refs):
        scale_ref, acc_ref, up_ref, down_ref, weight_ref, wct_ref = refs[:6]
        if last:
            earlier_ref, dy_ref, terms_ref, part_ref = refs[6:]
        else:
            dy_ref, terms_ref = refs[6:]
        sums = [jnp.zeros((STATE, HEAD_DIM), F32) for _ in range(heads)]
        if last:
            for b in range(2):
                for h in range(heads):
                    sums[h] = sums[h] + scale_ref[b, h] * earlier_ref[b, h]
        for b, piece in enumerate((up_ref, down_ref)):
            rows = slice(b * BLOCK, (b + 1) * BLOCK)
            dy = (acc_ref[rows, :] + dot(piece[...], weight_ref[...], NT)).astype(BF16)
            dy_ref[rows, :] = dy
            for h in range(heads):
                term = dot(wct_ref[b, h], dy[:, h * HEAD_DIM : (h + 1) * HEAD_DIM], NN)
                terms_ref[b, h] = term
                if last:
                    sums[h] = sums[h] + scale_ref[b + first, h] * term
        if last:
            for h in range(heads):
                part_ref[h] = sums[h]

    vmem = pl.BlockSpec(memory_space=pltpu.VMEM)
    wct = wct[first : first + 2]
    out_shape = [
        jax.ShapeDtypeStruct((tokens, width), BF16),
        jax.ShapeDtypeStruct((2, heads, STATE, HEAD_DIM), F32),
    ]
    in_specs = [pl.BlockSpec(memory_space=pltpu.SMEM)] + [vmem] * 5
    operands = [scale, acc, up, down, weight, wct]
    if last:
        out_shape.append(jax.ShapeDtypeStruct((heads, STATE, HEAD_DIM), F32))
        in_specs.append(vmem)
        operands.append(earlier)
    return pl.pallas_call(
        body,
        name="close_chunk",
        in_specs=in_specs,
        out_specs=[vmem] * len(out_shape),
        out_shape=out_shape,
        cost_estimate=pl.CostEstimate(flops=600_000_000, bytes_accessed=4_000_000, transcendentals=0),
        compiler_params=pltpu.CompilerParams(vmem_limit_bytes=VMEM_LIMIT),
    )(*operands)


def inside(first, dy, x, bc, sw, acol, dec, sct, spad, before):
    width = x.shape[1]
    tokens = x.shape[0]
    heads = width // HEAD_DIM

    def body(dy_ref, x_ref, bc_ref, sw_ref, acol_ref, dec_ref, sct_ref, spad_ref, *rest):
        dx_ref, dbc_ref, dlog_ref = rest[-3:]
        rows = lax.broadcasted_iota(jnp.int32, (BLOCK, BLOCK), 0)
        cols = lax.broadcasted_iota(jnp.int32, (BLOCK, BLOCK), 1)
        low = low_lanes((BLOCK, HEAD_DIM))
        for h in range(heads):
            lanes = slice(h * HEAD_DIM, (h + 1) * HEAD_DIM)
            dy_h = dy_ref[:, lanes]
            x_h = x_ref[:, lanes]
            bc_h = bc_ref[:, lanes]
            sw_h = sw_ref[:, lanes]
            zero = jnp.zeros_like(sw_h)
            gaps = dot(dy_h, x_h, NT)
            mixed = (gaps * dec_ref[0, h].astype(F32)).astype(BF16)
            dx_ref[:, lanes] = dot(sct_ref[0, h], dy_h, NN)
            grad = dot(mixed, jnp.where(low, zero, sw_h), NN)
            grad = grad + dot(mixed, jnp.where(low, sw_h, zero), TN)
            grad = grad + jnp.exp(acol_ref[:, lanes]) * dot(dy_h, spad_ref[0, h], NT)
            dbc_ref[:, lanes] = grad
            signed = grad * bc_h.astype(F32)
            moved = jnp.sum(jnp.where(low, -signed, signed), axis=1, keepdims=True)
            dlog_ref[h : h + 1, :] = jnp.sum(
                jnp.where(rows >= cols, moved, 0.0), axis=0, keepdims=True
            )

    def at(b):
        return (b + first, 0)

    def at4(b):
        return (b + first, 0, 0, 0)

    wide = pl.BlockSpec((BLOCK, width), at)
    square = pl.BlockSpec((1, heads, BLOCK, BLOCK), at4)
    in_specs = [
        pl.BlockSpec((BLOCK, width), lambda b: (b, 0)),
        wide,
        wide,
        wide,
        wide,
        square,
        square,
        pl.BlockSpec((1, heads, HEAD_DIM, HEAD_DIM), at4),
    ]
    operands = [dy, x, bc, sw, acol, dec, sct, spad]
    aliases = {}
    if before is not None:
        for place, array in enumerate(before):
            aliases[len(operands)] = place
            operands.append(array)
            in_specs.append(pl.BlockSpec(memory_space=pl.ANY))
    return pl.pallas_call(
        body,
        name="inside",
        grid=(2,),
        in_specs=in_specs,
        out_specs=[wide, wide, pl.BlockSpec((heads, BLOCK), lambda b: (0, b + first))],
        out_shape=[
            jax.ShapeDtypeStruct((tokens, width), F32),
            jax.ShapeDtypeStruct((tokens, width), F32),
            jax.ShapeDtypeStruct((heads, tokens), F32),
        ],
        input_output_aliases=aliases,
        cost_estimate=pl.CostEstimate(flops=2_000_000_000, bytes_accessed=7_000_000, transcendentals=0),
        compiler_params=pltpu.CompilerParams(vmem_limit_bytes=VMEM_LIMIT),
    )(*operands)


def finish(coefs, skip, a_last, received, dys, x, bc, acol, wb, terms, states, dx, dbc, dlog):
    tokens, width = x.shape
    heads = width // HEAD_DIM
    blocks = tokens // BLOCK
    count = len(received)

    def body(coefs_ref, skip_ref, last_ref, *refs):
        got = refs[:count]
        (dy0_ref, dy1_ref, x_ref, bc_ref, acol_ref, wb_ref, terms0_ref, terms1_ref, states_ref, dx_ref, dbc_ref,
         dlog_ref, out_ref, outbc_ref, outlog_ref, carry_ref) = refs[count:]
        step = pl.program_id(0)
        b = blocks - 1 - step

        @pl.when(step == 0)
        def _():
            for h in range(heads):
                total = coefs_ref[0, h] * got[0][h].astype(F32)
                for i in range(1, count):
                    total = total + coefs_ref[i, h] * got[i][h].astype(F32)
                carry_ref[h] = total

        rows = lax.broadcasted_iota(jnp.int32, (BLOCK, BLOCK), 0)
        cols = lax.broadcasted_iota(jnp.int32, (BLOCK, BLOCK), 1)
        late = step < 2
        for h in range(heads):
            lanes = slice(h * HEAD_DIM, (h + 1) * HEAD_DIM)
            carry = carry_ref[h]
            carry16 = carry.astype(BF16)
            dy_h = jnp.where(late, dy1_ref[:, lanes], dy0_ref[:, lanes]).astype(F32)
            grad = dx_ref[:, lanes] + dot(wb_ref[:, lanes][:, :STATE], carry16, NN)
            out_ref[:, lanes] = (grad + skip_ref[0, h] * dy_h).astype(BF16)
            padded = jnp.concatenate([carry16, jnp.zeros_like(carry16)], axis=0)
            last = last_ref[b, h]
            extra = jnp.exp(last - acol_ref[:, lanes]) * dot(x_ref[:, lanes], padded, NT)
            outbc_ref[:, lanes] = dbc_ref[:, lanes] + extra
            moved = jnp.sum(extra * bc_ref[:, lanes].astype(F32), axis=1, keepdims=True)
            ends = jnp.exp(jnp.full((1, HEAD_DIM), last, F32))
            whole = jnp.sum(jnp.sum(states_ref[0, h] * carry, axis=0, keepdims=True) * ends)
            outlog_ref[h : h + 1, :] = (
                dlog_ref[h : h + 1, :]
                + jnp.sum(jnp.where(rows < cols, moved, 0.0), axis=0, keepdims=True)
                + whole
            )
            carry_ref[h] = ends * carry + jnp.where(late, terms1_ref[0, h], terms0_ref[0, h])

    def at(i):
        return (blocks - 1 - i, 0)

    def at4(i):
        return (blocks - 1 - i, 0, 0, 0)

    wide = pl.BlockSpec((BLOCK, width), at)
    smem = pl.BlockSpec(memory_space=pltpu.SMEM)
    state_block = (1, heads, STATE, HEAD_DIM)
    line = pl.BlockSpec((heads, BLOCK), lambda i: (0, blocks - 1 - i))
    return pl.pallas_call(
        body,
        name="finish",
        grid=(blocks,),
        in_specs=[smem, smem, smem]
        + [pl.BlockSpec((heads, STATE, HEAD_DIM), lambda i: (0, 0, 0)) for _ in received]
        + [
            pl.BlockSpec((BLOCK, width), lambda i: (jnp.clip(3 - i, 0, 1), 0)),
            pl.BlockSpec((BLOCK, width), lambda i: (jnp.clip(1 - i, 0, 1), 0)),
            wide,
            wide,
            wide,
            wide,
            pl.BlockSpec(state_block, lambda i: (jnp.clip(3 - i, 0, 1), 0, 0, 0)),
            pl.BlockSpec(state_block, lambda i: (jnp.clip(1 - i, 0, 1), 0, 0, 0)),
            pl.BlockSpec(state_block, at4),
            wide,
            wide,
            line,
        ],
        out_specs=[wide, wide, line],
        out_shape=[
            jax.ShapeDtypeStruct((tokens, width), BF16),
            jax.ShapeDtypeStruct((tokens, width), F32),
            jax.ShapeDtypeStruct((heads, tokens), F32),
        ],
        scratch_shapes=[pltpu.VMEM((heads, STATE, HEAD_DIM), F32)],
        cost_estimate=pl.CostEstimate(flops=600_000_000, bytes_accessed=14_000_000, transcendentals=0),
        compiler_params=pltpu.CompilerParams(vmem_limit_bytes=VMEM_LIMIT),
    )(coefs, skip, a_last, *received, dys[0], dys[1], x, bc, acol, wb, terms[0], terms[1], states, dx, dbc, dlog)


def shift(count, by):
    return [(i, (i + by) % count) for i in range(count)]


def per_device(upstream, out_weight, inner_act, head_bc, log_decay, states, skip):
    tokens, width = inner_act.shape
    heads = log_decay.shape[0]
    blocks = tokens // BLOCK
    tp = lax.axis_size("tp")
    me = lax.axis_index("tp")
    ctx = lax.axis_index("ctx")
    feats = upstream.shape[1]
    px, py, pc = ctx // 8, (ctx // 2) % 4, ctx % 2

    logs = log_decay.reshape(heads, blocks, BLOCK)
    cum = jnp.cumsum(logs, axis=-1)
    last = cum[:, :, -1].T
    total = jnp.sum(last, axis=0)
    all_logs = lax.all_gather(jnp.zeros((8, 128), F32).at[0, :heads].set(total), "ctx")[:, 0, :heads]

    def weight_of(source):
        return lax.dynamic_slice_in_dim(out_weight, (source % tp) * feats, feats, 1)

    half = tokens // 2
    accs, lasts = [], []
    for c in range(2):
        own = upstream[c * half : (c + 1) * half]
        right = left = own
        acc = dot(own, weight_of(me), NT)
        for k in range(1, tp // 2):
            right = lax.ppermute(right, "tp", shift(tp, 1))
            left = lax.ppermute(left, "tp", shift(tp, -1))
            acc = acc + dot(right, weight_of(me - k + tp), NT) + dot(left, weight_of(me + k), NT)
        up = lax.ppermute(right[:BLOCK], "tp", shift(tp, 1))
        down = lax.ppermute(left[BLOCK:], "tp", shift(tp, -1))
        accs.append(acc)
        lasts.append((up, down))
    weight_last = weight_of(me + tp // 2)

    arow = cum.reshape(heads, tokens)
    acol = jnp.repeat(arow.T, HEAD_DIM, axis=1)
    swapped = head_bc.reshape(tokens, heads, 2, STATE)[:, :, ::-1, :].reshape(tokens, width)
    dec, sct, wct, wb = prepare(last, head_bc, swapped, arow, acol)
    spad = jnp.pad(states, ((0, 0), (0, 0), (STATE, 0), (0, 0))).astype(BF16)
    ahead = jnp.exp(jnp.cumsum(last, axis=0) - last)

    ids = jnp.arange(32)
    ix, iy, ic = ids // 8, (ids // 2) % 4, ids % 2
    row = ix == px
    chip = row & (iy == py)
    none = ids < 0
    after_core = chip & (ic > pc)
    after_y = row & (iy > py)
    yes = jnp.bool_(True)
    entries = [(chip & (ic == 0) & (pc == 1), yes), (chip & (ic == 0) & (pc == 0), yes)]
    entries.append((row & (iy < py), yes))
    for s in (1, 2, 3):
        sy = (py - s) % 4
        entries.append((row & (iy < sy), yes))
    finals = [(none, pc == 0)]
    for s in (1, 2, 3):
        sy = (py - s) % 4
        finals.append((after_core | (row & (iy > py) & (iy < sy)), sy > py))
    for s in (1, 2, 3):
        sx = (px - s) % 4
        finals.append((after_core | after_y | ((ix > px) & (ix < sx)), sx > px))
    entries = entries + finals
    masks = jnp.stack([m for m, _ in entries])
    valid = jnp.stack([v for _, v in entries])
    sums = jnp.sum(jnp.where(masks[:, :, None], all_logs[None], 0.0), axis=1)
    coefs = jnp.where(valid[:, None], jnp.exp(sums), 0.0)

    dy0, terms0 = close_chunk(0, accs[0], *lasts[0], weight_last, wct, ahead, None)
    dy1, terms1, part = close_chunk(2, accs[1], *lasts[1], weight_last, wct, ahead, terms0)

    def by(i):
        return coefs[i][:, None, None]

    places = [(x, y, c) for x in range(4) for y in range(4) for c in range(2)]

    def perm(dx, dy, dc):
        return [(x * 8 + y * 2 + c, ((x + dx) % 4) * 8 + ((y + dy) % 4) * 2 + (c ^ dc)) for x, y, c in places]

    part16 = part.astype(BF16)
    other = lax.ppermute(part16, "ctx", perm(0, 0, 1))
    chip_sum = (by(0) * part + by(1) * other.astype(F32)).astype(BF16)
    ys = [lax.ppermute(chip_sum, "ctx", perm(0, s, 0)) for s in (1, 2, 3)]
    dy0, chip_sum = lax.optimization_barrier((dy0, chip_sum))
    grads = inside(0, dy0, inner_act, head_bc, swapped, acol, dec, sct, spad, None)
    row_sum = by(2) * chip_sum.astype(F32)
    for s in range(3):
        row_sum = row_sum + by(3 + s) * ys[s].astype(F32)
    row_sum = row_sum.astype(BF16)
    xs = [lax.ppermute(row_sum, "ctx", perm(s, 0, 0)) for s in (1, 2, 3)]
    dy1, row_sum = lax.optimization_barrier((dy1, row_sum))
    dx, dbc, dlog = inside(2, dy1, inner_act, head_bc, swapped, acol, dec, sct, spad, grads)
    return finish(
        coefs[6:], skip[None], last, [other] + ys + xs, (dy0, dy1), inner_act, head_bc, acol, wb,
        (terms0, terms1), states, dx, dbc, dlog,
    )


def solution(mesh):
    return jax.shard_map(
        per_device,
        mesh=mesh,
        in_specs=(
            P("ctx", "tp"),
            P("tp", None),
            P("ctx", "tp"),
            P("ctx", "tp"),
            P("tp", "ctx"),
            P("ctx", "tp", None, None),
            P("tp"),
        ),
        out_specs=(P("ctx", "tp"), P("ctx", "tp"), P("tp", "ctx")),
        check_vma=False,
    )
```

```python
import jax
import jax.numpy as jnp
from jax import lax
from jax.experimental import pallas as pl
from jax.experimental.pallas import tpu as pltpu
from jax.sharding import PartitionSpec as P

HEAD_DIM = 128
STATE = 64
BLOCK = 256
F32 = jnp.float32
BF16 = jnp.bfloat16
VMEM_LIMIT = 20 << 20


def dot(a, b, dims):
    return lax.dot_general(a, b, (dims, ((), ())), preferred_element_type=F32)


NN = ((1,), (0,))
NT = ((1,), (1,))
TN = ((0,), (0,))


def low_lanes(shape):
    return lax.broadcasted_iota(jnp.int32, shape, len(shape) - 1) < STATE


def prepare_kernel(heads, bc_ref, sw_ref, arow_ref, acol_ref, dec_ref, sct_ref, wct_ref):
    rows = lax.broadcasted_iota(jnp.int32, (BLOCK, BLOCK), 0)
    cols = lax.broadcasted_iota(jnp.int32, (BLOCK, BLOCK), 1)
    low = low_lanes((BLOCK, HEAD_DIM))
    for h in range(heads):
        lanes = slice(h * HEAD_DIM, (h + 1) * HEAD_DIM)
        row = arow_ref[h : h + 1, :]
        col1 = acol_ref[:, lanes]
        col = jnp.concatenate([col1, col1], axis=1)
        gap = col - row
        dec_ref[0, h] = jnp.where(rows >= cols, jnp.exp(jnp.minimum(gap, 0.0)), 0.0).astype(BF16)
        bc = bc_ref[:, lanes]
        sw = sw_ref[:, lanes]
        zero = jnp.zeros_like(bc)
        c_low = jnp.where(low, sw, zero)
        b_low = jnp.where(low, bc, zero)
        scores = dot(b_low, c_low, NT)
        back = jnp.where(cols >= rows, jnp.exp(jnp.minimum(-gap, 0.0)), 0.0)
        sct_ref[0, h] = (scores * back).astype(BF16)
        weighted = c_low.astype(F32) * jnp.exp(col1)
        wct_ref[0, h] = weighted.T[:STATE, :].astype(BF16)


def prepare_body(heads):
    def body(*refs):
        prepare_kernel(heads, *refs)

    return body


def prepare(bc, sw, arow, acol):
    tokens, width = bc.shape
    heads = width // HEAD_DIM
    blocks = tokens // BLOCK
    wide = pl.BlockSpec((BLOCK, width), lambda b: (b, 0))
    square = pl.BlockSpec((1, heads, BLOCK, BLOCK), lambda b: (b, 0, 0, 0))
    return pl.pallas_call(
        prepare_body(heads),
        name="prepare",
        grid=(blocks,),
        in_specs=[
            wide,
            wide,
            pl.BlockSpec((heads, BLOCK), lambda b: (0, b)),
            wide,
        ],
        out_specs=[
            square,
            square,
            pl.BlockSpec((1, heads, STATE, BLOCK), lambda b: (b, 0, 0, 0)),
        ],
        out_shape=[
            jax.ShapeDtypeStruct((blocks, heads, BLOCK, BLOCK), BF16),
            jax.ShapeDtypeStruct((blocks, heads, BLOCK, BLOCK), BF16),
            jax.ShapeDtypeStruct((blocks, heads, STATE, BLOCK), BF16),
        ],
        cost_estimate=pl.CostEstimate(flops=4_000_000_000, bytes_accessed=9_000_000, transcendentals=0),
        compiler_params=pltpu.CompilerParams(vmem_limit_bytes=VMEM_LIMIT),
    )(bc, sw, arow, acol)


def close_chunk(first, acc, up, down, weight, wct, scale, earlier):
    tokens, width = acc.shape
    heads = width // HEAD_DIM
    last = earlier is not None

    def body(*refs):
        scale_ref, acc_ref, up_ref, down_ref, weight_ref, wct_ref = refs[:6]
        if last:
            earlier_ref, dy_ref, terms_ref, part_ref = refs[6:]
        else:
            dy_ref, terms_ref = refs[6:]
        sums = [jnp.zeros((STATE, HEAD_DIM), F32) for _ in range(heads)]
        if last:
            for b in range(2):
                for h in range(heads):
                    sums[h] = sums[h] + scale_ref[b, h] * earlier_ref[b, h]
        for b, piece in enumerate((up_ref, down_ref)):
            rows = slice(b * BLOCK, (b + 1) * BLOCK)
            dy = (acc_ref[rows, :] + dot(piece[...], weight_ref[...], NT)).astype(BF16)
            dy_ref[rows, :] = dy
            for h in range(heads):
                term = dot(wct_ref[b, h], dy[:, h * HEAD_DIM : (h + 1) * HEAD_DIM], NN)
                terms_ref[b, h] = term
                if last:
                    sums[h] = sums[h] + scale_ref[b + first, h] * term
        if last:
            for h in range(heads):
                part_ref[h] = sums[h]

    vmem = pl.BlockSpec(memory_space=pltpu.VMEM)
    wct = wct[first : first + 2]
    out_shape = [
        jax.ShapeDtypeStruct((tokens, width), BF16),
        jax.ShapeDtypeStruct((2, heads, STATE, HEAD_DIM), F32),
    ]
    in_specs = [pl.BlockSpec(memory_space=pltpu.SMEM)] + [vmem] * 5
    operands = [scale, acc, up, down, weight, wct]
    if last:
        out_shape.append(jax.ShapeDtypeStruct((heads, STATE, HEAD_DIM), F32))
        in_specs.append(vmem)
        operands.append(earlier)
    return pl.pallas_call(
        body,
        name="close_chunk",
        in_specs=in_specs,
        out_specs=[vmem] * len(out_shape),
        out_shape=out_shape,
        cost_estimate=pl.CostEstimate(flops=600_000_000, bytes_accessed=4_000_000, transcendentals=0),
        compiler_params=pltpu.CompilerParams(vmem_limit_bytes=VMEM_LIMIT),
    )(*operands)


def inside(first, count, dy_first, dy, skip, x, bc, sw, acol, dec, sct, spad, before):
    tokens, width = x.shape
    heads = width // HEAD_DIM
    group = heads // 2

    def body(skip_ref, dy_ref, x_ref, bc_ref, sw_ref, acol_ref, dec_ref, sct_ref, spad_ref, *rest):
        dx_ref, dbc_ref, dlog_ref = rest[-3:]
        base = pl.program_id(1) * group
        rows = lax.broadcasted_iota(jnp.int32, (BLOCK, BLOCK), 0)
        cols = lax.broadcasted_iota(jnp.int32, (BLOCK, BLOCK), 1)
        low = low_lanes((BLOCK, HEAD_DIM))
        for h in range(group):
            lanes = slice(h * HEAD_DIM, (h + 1) * HEAD_DIM)
            dy_h = dy_ref[:, lanes]
            x_h = x_ref[:, lanes]
            bc_h = bc_ref[:, lanes]
            sw_h = sw_ref[:, lanes]
            zero = jnp.zeros_like(sw_h)
            gaps = dot(dy_h, x_h, NT)
            mixed = (gaps * dec_ref[0, h].astype(F32)).astype(BF16)
            dx_ref[:, lanes] = dot(sct_ref[0, h], dy_h, NN) + skip_ref[0, base + h] * dy_h.astype(F32)
            grad = dot(mixed, jnp.where(low, zero, sw_h), NN)
            grad = grad + dot(mixed, jnp.where(low, sw_h, zero), TN)
            grad = grad + jnp.exp(acol_ref[:, lanes]) * dot(dy_h, spad_ref[0, h], NT)
            dbc_ref[:, lanes] = grad
            signed = grad * bc_h.astype(F32)
            moved = jnp.sum(jnp.where(low, -signed, signed), axis=1, keepdims=True)
            dlog_ref[h] = jnp.sum(jnp.where(rows >= cols, moved, 0.0), axis=0, keepdims=True)

    wide = pl.BlockSpec((BLOCK, group * HEAD_DIM), lambda b, g: (b + first, g))
    square = pl.BlockSpec((1, group, BLOCK, BLOCK), lambda b, g: (b + first, g, 0, 0))
    in_specs = [
        pl.BlockSpec(memory_space=pltpu.SMEM),
        pl.BlockSpec((BLOCK, group * HEAD_DIM), lambda b, g: (b + dy_first, g)),
        wide,
        wide,
        wide,
        wide,
        square,
        square,
        pl.BlockSpec((1, group, HEAD_DIM, HEAD_DIM), lambda b, g: (b + first, g, 0, 0)),
    ]
    operands = [skip, dy, x, bc, sw, acol, dec, sct, spad]
    aliases = {}
    if before is not None:
        for place, array in enumerate(before):
            aliases[len(operands)] = place
            operands.append(array)
            in_specs.append(pl.BlockSpec(memory_space=pl.ANY))
    return pl.pallas_call(
        body,
        name="inside",
        grid=(count, 2),
        in_specs=in_specs,
        out_specs=[wide, wide, pl.BlockSpec((group, 1, BLOCK), lambda b, g: (g, 0, b + first))],
        out_shape=[
            jax.ShapeDtypeStruct((tokens, width), F32),
            jax.ShapeDtypeStruct((tokens, width), F32),
            jax.ShapeDtypeStruct((heads, 1, tokens), F32),
        ],
        input_output_aliases=aliases,
        cost_estimate=pl.CostEstimate(
            flops=1_000_000_000 * count, bytes_accessed=3_500_000 * count, transcendentals=0
        ),
        compiler_params=pltpu.CompilerParams(vmem_limit_bytes=VMEM_LIMIT),
    )(*operands)


def finish(coefs, a_last, received, x, bc, aline, terms, states, dx, dbc, dlog):
    tokens, width = x.shape
    heads = width // HEAD_DIM
    blocks = tokens // BLOCK
    count = len(received)

    def body(coefs_ref, last_ref, *refs):
        got = refs[:count]
        (x_ref, bc_ref, aline_ref, terms0_ref, terms1_ref, states_ref, dx_ref, dbc_ref, dlog_ref, out_ref,
         outbc_ref, outlog_ref, carry_ref) = refs[count:]
        step = pl.program_id(0)
        b = blocks - 1 - step

        @pl.when(step == 0)
        def _():
            for h in range(heads):
                total = coefs_ref[0, h] * got[0][h].astype(F32)
                for i in range(1, count):
                    total = total + coefs_ref[i, h] * got[i][h].astype(F32)
                carry_ref[h] = total

        rows = lax.broadcasted_iota(jnp.int32, (BLOCK, BLOCK), 0)
        cols = lax.broadcasted_iota(jnp.int32, (BLOCK, BLOCK), 1)
        late = step < blocks // 2
        for h in range(heads):
            lanes = slice(h * HEAD_DIM, (h + 1) * HEAD_DIM)
            carry = carry_ref[h]
            carry16 = carry.astype(BF16)
            last = last_ref[b, h]
            tail = jnp.exp(last - aline_ref[:, h : h + 1])
            bc_h = bc_ref[:, lanes].astype(F32)
            weighted = (bc_h * tail).astype(BF16)[:, :STATE]
            out_ref[:, lanes] = (dx_ref[:, lanes] + dot(weighted, carry16, NN)).astype(BF16)
            padded = jnp.concatenate([carry16, jnp.zeros_like(carry16)], axis=0)
            extra = tail * dot(x_ref[:, lanes], padded, NT)
            outbc_ref[:, lanes] = dbc_ref[:, lanes] + extra
            moved = jnp.sum(extra * bc_h, axis=1, keepdims=True)
            ends = jnp.exp(jnp.full((1, HEAD_DIM), last, F32))
            whole = jnp.sum(jnp.sum(states_ref[0, h] * carry, axis=0, keepdims=True) * ends)
            outlog_ref[h : h + 1, :] = (
                dlog_ref[h] + jnp.sum(jnp.where(rows < cols, moved, 0.0), axis=0, keepdims=True) + whole
            )
            carry_ref[h] = ends * carry + jnp.where(late, terms1_ref[0, h], terms0_ref[0, h])

    wide = pl.BlockSpec((BLOCK, width), lambda i: (blocks - 1 - i, 0))
    smem = pl.BlockSpec(memory_space=pltpu.SMEM)
    state_block = (1, heads, STATE, HEAD_DIM)
    half = blocks // 2
    return pl.pallas_call(
        body,
        name="finish",
        grid=(blocks,),
        in_specs=[smem, smem]
        + [pl.BlockSpec((heads, STATE, HEAD_DIM), lambda i: (0, 0, 0)) for _ in received]
        + [
            wide,
            wide,
            pl.BlockSpec((BLOCK, heads), lambda i: (blocks - 1 - i, 0)),
            pl.BlockSpec(state_block, lambda i: (jnp.clip(blocks - 1 - i, 0, half - 1), 0, 0, 0)),
            pl.BlockSpec(state_block, lambda i: (jnp.clip(half - 1 - i, 0, half - 1), 0, 0, 0)),
            pl.BlockSpec(state_block, lambda i: (blocks - 1 - i, 0, 0, 0)),
            wide,
            wide,
            pl.BlockSpec((heads, 1, BLOCK), lambda i: (0, 0, blocks - 1 - i)),
        ],
        out_specs=[wide, wide, pl.BlockSpec((heads, BLOCK), lambda i: (0, blocks - 1 - i))],
        out_shape=[
            jax.ShapeDtypeStruct((tokens, width), BF16),
            jax.ShapeDtypeStruct((tokens, width), F32),
            jax.ShapeDtypeStruct((heads, tokens), F32),
        ],
        scratch_shapes=[pltpu.VMEM((heads, STATE, HEAD_DIM), F32)],
        cost_estimate=pl.CostEstimate(flops=600_000_000, bytes_accessed=11_000_000, transcendentals=0),
        compiler_params=pltpu.CompilerParams(vmem_limit_bytes=VMEM_LIMIT),
    )(coefs, a_last, *received, x, bc, aline, terms[0], terms[1], states, dx, dbc, dlog)


def shift(count, by):
    return [(i, (i + by) % count) for i in range(count)]


def per_device(upstream, out_weight, inner_act, head_bc, log_decay, states, skip):
    tokens, width = inner_act.shape
    heads = log_decay.shape[0]
    blocks = tokens // BLOCK
    tp = lax.axis_size("tp")
    me = lax.axis_index("tp")
    ctx = lax.axis_index("ctx")
    feats = upstream.shape[1]
    px, py, pc = ctx // 8, (ctx // 2) % 4, ctx % 2

    logs = log_decay.reshape(heads, blocks, BLOCK)
    cum = jnp.cumsum(logs, axis=-1)
    last = cum[:, :, -1].T
    total = jnp.sum(last, axis=0)
    all_logs = lax.all_gather(jnp.zeros((64, 128), F32).at[0, :heads].set(total), "ctx")[:, 0, :heads]

    def weight_of(source):
        return lax.dynamic_slice_in_dim(out_weight, (source % tp) * feats, feats, 1)

    half = tokens // 2
    accs, lasts = [], []
    for c in range(2):
        own = upstream[c * half : (c + 1) * half]
        if c == 0:
            upstream, _ = lax.optimization_barrier((upstream, own))
        right = left = own
        acc = dot(own, weight_of(me), NT)
        for k in range(1, tp // 2):
            right = lax.ppermute(right, "tp", shift(tp, 1))
            left = lax.ppermute(left, "tp", shift(tp, -1))
            acc = acc + dot(right, weight_of(me - k + tp), NT) + dot(left, weight_of(me + k), NT)
        up = lax.ppermute(right[:BLOCK], "tp", shift(tp, 1))
        down = lax.ppermute(left[BLOCK:], "tp", shift(tp, -1))
        accs.append(acc)
        lasts.append((up, down))
    weight_last = weight_of(me + tp // 2)

    arow = cum.reshape(heads, tokens)
    aline = arow.T
    acol = jnp.repeat(aline, HEAD_DIM, axis=1)
    swapped = head_bc.reshape(tokens, heads, 2, STATE)[:, :, ::-1, :].reshape(tokens, width)
    dec, sct, wct = prepare(head_bc, swapped, arow, acol)
    spad = jnp.pad(states, ((0, 0), (0, 0), (STATE, 0), (0, 0))).astype(BF16)
    ahead = jnp.exp(jnp.cumsum(last, axis=0) - last)

    ids = jnp.arange(32)
    ix, iy, ic = ids // 8, (ids // 2) % 4, ids % 2
    row = ix == px
    chip = row & (iy == py)
    none = ids < 0
    after_core = chip & (ic > pc)
    after_y = row & (iy > py)
    yes = jnp.bool_(True)
    entries = [(chip & (ic == 0) & (pc == 1), yes), (chip & (ic == 0) & (pc == 0), yes)]
    entries.append((row & (iy < py), yes))
    for s in (1, 2, 3):
        sy = (py - s) % 4
        entries.append((row & (iy < sy), yes))
    finals = [(none, pc == 0)]
    for s in (1, 2, 3):
        sy = (py - s) % 4
        finals.append((after_core | (row & (iy > py) & (iy < sy)), sy > py))
    for s in (1, 2, 3):
        sx = (px - s) % 4
        finals.append((after_core | after_y | ((ix > px) & (ix < sx)), sx > px))
    entries = entries + finals
    masks = jnp.stack([m for m, _ in entries])
    valid = jnp.stack([v for _, v in entries])
    sums = jnp.sum(jnp.where(masks[:, :, None], all_logs[None], 0.0), axis=1)
    coefs = jnp.where(valid[:, None], jnp.exp(sums), 0.0)

    skips = skip[None]

    def within(first, count, dy_first, dy, before):
        return inside(
            first, count, dy_first, dy, skips, inner_act, head_bc, swapped, acol, dec, sct, spad, before
        )

    dy0, terms0 = close_chunk(0, accs[0], *lasts[0], weight_last, wct, ahead, None)
    grads = within(0, 2, 0, dy0, None)
    lasts[1], coefs, grads = lax.optimization_barrier((lasts[1], coefs, grads))
    dy1, terms1, part = close_chunk(2, accs[1], *lasts[1], weight_last, wct, ahead, terms0)

    def by(i):
        return coefs[i][:, None, None]

    places = [(x, y, c) for x in range(4) for y in range(4) for c in range(2)]

    def perm(dx, dy, dc):
        return [(x * 8 + y * 2 + c, ((x + dx) % 4) * 8 + ((y + dy) % 4) * 2 + (c ^ dc)) for x, y, c in places]

    part16 = part.astype(BF16)
    other = lax.ppermute(part16, "ctx", perm(0, 0, 1))
    chip_sum = (by(0) * part + by(1) * other.astype(F32)).astype(BF16)
    ys = [lax.ppermute(chip_sum, "ctx", perm(0, s, 0)) for s in (1, 2, 3)]
    dy1, chip_sum = lax.optimization_barrier((dy1, chip_sum))
    grads = within(2, 1, 0, dy1, grads)
    row_sum = by(2) * chip_sum.astype(F32)
    for s in range(3):
        row_sum = row_sum + by(3 + s) * ys[s].astype(F32)
    row_sum = row_sum.astype(BF16)
    xs = [lax.ppermute(row_sum, "ctx", perm(s, 0, 0)) for s in (1, 2, 3)]
    dy1, row_sum = lax.optimization_barrier((dy1, row_sum))
    dx, dbc, dlog = within(3, 1, 1, dy1, grads)
    return finish(
        coefs[6:], last, [other] + ys + xs, inner_act, head_bc, aline, (terms0, terms1), states, dx, dbc, dlog
    )


def solution(mesh):
    return jax.shard_map(
        per_device,
        mesh=mesh,
        in_specs=(
            P("ctx", "tp"),
            P("tp", None),
            P("ctx", "tp"),
            P("ctx", "tp"),
            P("tp", "ctx"),
            P("ctx", "tp", None, None),
            P("tp"),
        ),
        out_specs=(P("ctx", "tp"), P("ctx", "tp"), P("tp", "ctx")),
        check_vma=False,
    )
```

```python
import jax
import jax.numpy as jnp
from jax import lax
from jax.experimental import pallas as pl
from jax.experimental.pallas import tpu as pltpu
from jax.sharding import PartitionSpec as P

HEAD_DIM = 128
STATE = 64
BLOCK = 256
F32 = jnp.float32
BF16 = jnp.bfloat16
VMEM_LIMIT = 60 << 20


def dot(a, b, dims):
    return lax.dot_general(a, b, (dims, ((), ())), preferred_element_type=F32)


NN = ((1,), (0,))
NT = ((1,), (1,))
TN = ((0,), (0,))


def low_lanes(shape):
    return lax.broadcasted_iota(jnp.int32, shape, len(shape) - 1) < STATE


def prepare(bc, arow, aline, states):
    tokens, width = bc.shape
    heads = width // HEAD_DIM
    blocks = tokens // BLOCK

    def body(bc_ref, arow_ref, aline_ref, states_ref, sw_ref, dec_ref, sct_ref, wct_ref, spad_ref):
        rows = lax.broadcasted_iota(jnp.int32, (BLOCK, BLOCK), 0)
        cols = lax.broadcasted_iota(jnp.int32, (BLOCK, BLOCK), 1)
        low = low_lanes((BLOCK, HEAD_DIM))
        for h in range(heads):
            lanes = slice(h * HEAD_DIM, (h + 1) * HEAD_DIM)
            gap = aline_ref[:, h : h + 1] - arow_ref[h : h + 1, :]
            dec_ref[0, h] = jnp.where(rows >= cols, jnp.exp(jnp.minimum(gap, 0.0)), 0.0).astype(BF16)
            bc = bc_ref[:, lanes].astype(F32)
            swapped = pltpu.roll(bc, STATE, 1)
            sw_ref[:, lanes] = swapped.astype(BF16)
            c_low = jnp.where(low, swapped, 0.0)
            b_low = jnp.where(low, bc, 0.0)
            scores = dot(b_low.astype(BF16), c_low.astype(BF16), NT)
            back = jnp.where(cols >= rows, jnp.exp(jnp.minimum(-gap, 0.0)), 0.0)
            sct_ref[0, h] = (scores * back).astype(BF16)
            weighted = c_low * jnp.exp(aline_ref[:, h : h + 1])
            wct_ref[0, h] = weighted.T[:STATE, :].astype(BF16)
            state = states_ref[0, h].astype(BF16)
            spad_ref[0, h] = jnp.concatenate([jnp.zeros_like(state), state], axis=0)

    wide = pl.BlockSpec((BLOCK, width), lambda b: (b, 0))

    def block4(*dims):
        return pl.BlockSpec((1, heads) + dims, lambda b: (b, 0, 0, 0))

    return pl.pallas_call(
        body,
        name="prepare",
        grid=(blocks,),
        in_specs=[
            wide,
            pl.BlockSpec((heads, BLOCK), lambda b: (0, b)),
            pl.BlockSpec((BLOCK, heads), lambda b: (b, 0)),
            block4(STATE, HEAD_DIM),
        ],
        out_specs=[
            wide,
            block4(BLOCK, BLOCK),
            block4(BLOCK, BLOCK),
            block4(STATE, BLOCK),
            block4(HEAD_DIM, HEAD_DIM),
        ],
        out_shape=[
            jax.ShapeDtypeStruct((tokens, width), BF16),
            jax.ShapeDtypeStruct((blocks, heads, BLOCK, BLOCK), BF16),
            jax.ShapeDtypeStruct((blocks, heads, BLOCK, BLOCK), BF16),
            jax.ShapeDtypeStruct((blocks, heads, STATE, BLOCK), BF16),
            jax.ShapeDtypeStruct((blocks, heads, HEAD_DIM, HEAD_DIM), BF16),
        ],
        cost_estimate=pl.CostEstimate(flops=4_000_000_000, bytes_accessed=9_000_000, transcendentals=0),
        compiler_params=pltpu.CompilerParams(vmem_limit_bytes=VMEM_LIMIT),
    )(bc, arow, aline, states)


def close_chunk(first, source, acc, up, down, weight, wct, scale, earlier):
    tokens, width = acc.shape
    heads = width // HEAD_DIM
    last = earlier is not None

    def body(source_ref, *refs):
        scale_ref, acc_ref, up_ref, down_ref, weight_ref, wct_ref = refs[:6]
        if last:
            earlier_ref, dy_ref, terms_ref, part_ref = refs[6:]
        else:
            dy_ref, terms_ref = refs[6:]
        sums = [jnp.zeros((STATE, HEAD_DIM), F32) for _ in range(heads)]
        if last:
            for b in range(2):
                for h in range(heads):
                    sums[h] = sums[h] + scale_ref[b, h] * earlier_ref[b, h]
        for b, piece in enumerate((up_ref, down_ref)):
            rows = slice(b * BLOCK, (b + 1) * BLOCK)
            dy = (acc_ref[rows, :] + dot(piece[...], weight_ref[...], NT)).astype(BF16)
            dy_ref[rows, :] = dy
            for h in range(heads):
                term = dot(wct_ref[b, h], dy[:, h * HEAD_DIM : (h + 1) * HEAD_DIM], NN)
                terms_ref[b, h] = term
                if last:
                    sums[h] = sums[h] + scale_ref[b + first, h] * term
        if last:
            for h in range(heads):
                part_ref[h] = sums[h]

    def whole(*dims):
        return pl.BlockSpec(dims, lambda i, source: (0,) * len(dims))

    terms_shape = (2, heads, STATE, HEAD_DIM)
    out_shape = [jax.ShapeDtypeStruct((tokens, width), BF16), jax.ShapeDtypeStruct(terms_shape, F32)]
    out_specs = [whole(tokens, width), whole(*terms_shape)]
    in_specs = [
        pl.BlockSpec(memory_space=pltpu.SMEM),
        whole(tokens, width),
        whole(*up.shape),
        whole(*down.shape),
        pl.BlockSpec((width, up.shape[1]), lambda i, source: (0, source[0])),
        pl.BlockSpec((2, heads, STATE, BLOCK), lambda i, source: (first // 2, 0, 0, 0)),
    ]
    operands = [scale, acc, up, down, weight, wct]
    if last:
        out_shape.append(jax.ShapeDtypeStruct((heads, STATE, HEAD_DIM), F32))
        out_specs.append(whole(heads, STATE, HEAD_DIM))
        in_specs.append(whole(*terms_shape))
        operands.append(earlier)
    return pl.pallas_call(
        body,
        name="close_chunk",
        grid_spec=pltpu.PrefetchScalarGridSpec(
            num_scalar_prefetch=1, grid=(1,), in_specs=in_specs, out_specs=out_specs
        ),
        out_shape=out_shape,
        cost_estimate=pl.CostEstimate(flops=600_000_000, bytes_accessed=4_000_000, transcendentals=0),
        compiler_params=pltpu.CompilerParams(vmem_limit_bytes=VMEM_LIMIT),
    )(source, *operands)


def inside(first, count, dy_first, dy, skip, x, bc, sw, aline, dec, sct, spad, before):
    tokens, width = x.shape
    heads = width // HEAD_DIM
    group = heads // 2

    def body(skip_ref, dy_ref, x_ref, bc_ref, sw_ref, aline_ref, dec_ref, sct_ref, spad_ref, *rest):
        dx_ref, dbc_ref, dlog_ref = rest[-3:]
        base = pl.program_id(1) * group
        rows = lax.broadcasted_iota(jnp.int32, (BLOCK, BLOCK), 0)
        cols = lax.broadcasted_iota(jnp.int32, (BLOCK, BLOCK), 1)
        low = low_lanes((BLOCK, HEAD_DIM))
        for h in range(group):
            lanes = slice(h * HEAD_DIM, (h + 1) * HEAD_DIM)
            dy_h = dy_ref[:, lanes]
            x_h = x_ref[:, lanes]
            bc_h = bc_ref[:, lanes]
            sw_h = sw_ref[:, lanes]
            zero = jnp.zeros_like(sw_h)
            gaps = dot(dy_h, x_h, NT)
            mixed = (gaps * dec_ref[0, h].astype(F32)).astype(BF16)
            dx_ref[:, lanes] = dot(sct_ref[0, h], dy_h, NN) + skip_ref[0, base + h] * dy_h.astype(F32)
            grad = dot(mixed, jnp.where(low, zero, sw_h), NN)
            grad = grad + dot(mixed, jnp.where(low, sw_h, zero), TN)
            grad = grad + jnp.exp(aline_ref[0][:, h : h + 1]) * dot(dy_h, spad_ref[0, h], NT)
            dbc_ref[:, lanes] = grad
            signed = grad * bc_h.astype(F32)
            moved = jnp.sum(jnp.where(low, -signed, signed), axis=1, keepdims=True)
            dlog_ref[h] = jnp.sum(jnp.where(rows >= cols, moved, 0.0), axis=0, keepdims=True)

    wide = pl.BlockSpec((BLOCK, group * HEAD_DIM), lambda b, g: (b + first, g))
    square = pl.BlockSpec((1, group, BLOCK, BLOCK), lambda b, g: (b + first, g, 0, 0))
    in_specs = [
        pl.BlockSpec(memory_space=pltpu.SMEM),
        pl.BlockSpec((BLOCK, group * HEAD_DIM), lambda b, g: (b + dy_first, g)),
        wide,
        wide,
        wide,
        pl.BlockSpec((1, BLOCK, group), lambda b, g: (g, b + first, 0)),
        square,
        square,
        pl.BlockSpec((1, group, HEAD_DIM, HEAD_DIM), lambda b, g: (b + first, g, 0, 0)),
    ]
    operands = [skip, dy, x, bc, sw, jnp.stack([aline[:, :group], aline[:, group:]]), dec, sct, spad]
    aliases = {}
    if before is not None:
        for place, array in enumerate(before):
            aliases[len(operands)] = place
            operands.append(array)
            in_specs.append(pl.BlockSpec(memory_space=pl.ANY))
    return pl.pallas_call(
        body,
        name="inside",
        grid=(count, 2),
        in_specs=in_specs,
        out_specs=[wide, wide, pl.BlockSpec((group, 1, BLOCK), lambda b, g: (g, 0, b + first))],
        out_shape=[
            jax.ShapeDtypeStruct((tokens, width), F32),
            jax.ShapeDtypeStruct((tokens, width), F32),
            jax.ShapeDtypeStruct((heads, 1, tokens), F32),
        ],
        input_output_aliases=aliases,
        cost_estimate=pl.CostEstimate(
            flops=1_000_000_000 * count, bytes_accessed=3_500_000 * count, transcendentals=0
        ),
        compiler_params=pltpu.CompilerParams(vmem_limit_bytes=VMEM_LIMIT),
    )(*operands)


def finish(coefs, a_last, received, x, bc, aline, terms, states, dx, dbc, dlog):
    tokens, width = x.shape
    heads = width // HEAD_DIM
    blocks = tokens // BLOCK
    count = len(received)

    def body(coefs_ref, last_ref, *refs):
        got = refs[:count]
        (x_ref, bc_ref, aline_ref, terms0_ref, terms1_ref, states_ref, dx_ref, dbc_ref, dlog_ref, out_ref,
         outbc_ref, outlog_ref, carry_ref) = refs[count:]
        step = pl.program_id(0)
        b = blocks - 1 - step

        @pl.when(step == 0)
        def _():
            for h in range(heads):
                total = coefs_ref[0, h] * got[0][h].astype(F32)
                for i in range(1, count):
                    total = total + coefs_ref[i, h] * got[i][h].astype(F32)
                carry_ref[h] = total

        rows = lax.broadcasted_iota(jnp.int32, (BLOCK, BLOCK), 0)
        cols = lax.broadcasted_iota(jnp.int32, (BLOCK, BLOCK), 1)
        late = step < blocks // 2
        for h in range(heads):
            lanes = slice(h * HEAD_DIM, (h + 1) * HEAD_DIM)
            carry = carry_ref[h]
            carry16 = carry.astype(BF16)
            last = last_ref[b, h]
            tail = jnp.exp(last - aline_ref[:, h : h + 1])
            bc_h = bc_ref[:, lanes].astype(F32)
            weighted = (bc_h * tail).astype(BF16)[:, :STATE]
            out_ref[:, lanes] = (dx_ref[:, lanes] + dot(weighted, carry16, NN)).astype(BF16)
            padded = jnp.concatenate([carry16, jnp.zeros_like(carry16)], axis=0)
            extra = tail * dot(x_ref[:, lanes], padded, NT)
            outbc_ref[:, lanes] = dbc_ref[:, lanes] + extra
            moved = jnp.sum(extra * bc_h, axis=1, keepdims=True)
            ends = jnp.exp(jnp.full((1, HEAD_DIM), last, F32))
            whole = jnp.sum(jnp.sum(states_ref[0, h] * carry, axis=0, keepdims=True) * ends)
            outlog_ref[h : h + 1, :] = (
                dlog_ref[h] + jnp.sum(jnp.where(rows < cols, moved, 0.0), axis=0, keepdims=True) + whole
            )
            carry_ref[h] = ends * carry + jnp.where(late, terms1_ref[0, h], terms0_ref[0, h])

    wide = pl.BlockSpec((BLOCK, width), lambda i: (blocks - 1 - i, 0))
    smem = pl.BlockSpec(memory_space=pltpu.SMEM)
    state_block = (1, heads, STATE, HEAD_DIM)
    half = blocks // 2
    return pl.pallas_call(
        body,
        name="finish",
        grid=(blocks,),
        in_specs=[smem, smem]
        + [pl.BlockSpec((heads, STATE, HEAD_DIM), lambda i: (0, 0, 0)) for _ in received]
        + [
            wide,
            wide,
            pl.BlockSpec((BLOCK, heads), lambda i: (blocks - 1 - i, 0)),
            pl.BlockSpec(state_block, lambda i: (jnp.clip(blocks - 1 - i, 0, half - 1), 0, 0, 0)),
            pl.BlockSpec(state_block, lambda i: (jnp.clip(half - 1 - i, 0, half - 1), 0, 0, 0)),
            pl.BlockSpec(state_block, lambda i: (blocks - 1 - i, 0, 0, 0)),
            wide,
            wide,
            pl.BlockSpec((heads, 1, BLOCK), lambda i: (0, 0, blocks - 1 - i)),
        ],
        out_specs=[wide, wide, pl.BlockSpec((heads, BLOCK), lambda i: (0, blocks - 1 - i))],
        out_shape=[
            jax.ShapeDtypeStruct((tokens, width), BF16),
            jax.ShapeDtypeStruct((tokens, width), F32),
            jax.ShapeDtypeStruct((heads, tokens), F32),
        ],
        scratch_shapes=[pltpu.VMEM((heads, STATE, HEAD_DIM), F32)],
        cost_estimate=pl.CostEstimate(flops=600_000_000, bytes_accessed=11_000_000, transcendentals=0),
        compiler_params=pltpu.CompilerParams(vmem_limit_bytes=VMEM_LIMIT),
    )(coefs, a_last, *received, x, bc, aline, terms[0], terms[1], states, dx, dbc, dlog)


def shift(count, by):
    return [(i, (i + by) % count) for i in range(count)]


def per_device(upstream, out_weight, inner_act, head_bc, log_decay, states, skip):
    tokens, width = inner_act.shape
    heads = log_decay.shape[0]
    blocks = tokens // BLOCK
    tp = lax.axis_size("tp")
    me = lax.axis_index("tp")
    ctx = lax.axis_index("ctx")
    feats = upstream.shape[1]
    px, py, pc = ctx // 8, (ctx // 2) % 4, ctx % 2

    places = [(x, y, c) for x in range(4) for y in range(4) for c in range(2)]

    def perm(dx, dy, dc):
        return [(x * 8 + y * 2 + c, ((x + dx) % 4) * 8 + ((y + dy) % 4) * 2 + (c ^ dc)) for x, y, c in places]

    def from_core(a):
        return lax.ppermute(a, "ctx", perm(0, 0, 1))

    def from_y(a):
        return [lax.ppermute(a, "ctx", perm(0, s, 0)) for s in (1, 2, 3)]

    def from_x(a):
        return [lax.ppermute(a, "ctx", perm(s, 0, 0)) for s in (1, 2, 3)]

    def weight_of(source):
        return lax.dynamic_slice_in_dim(out_weight, (source % tp) * feats, feats, 1)

    half = tokens // 2
    accs, lasts, firsts, seconds = [], [], [], []
    for c in range(2):
        own = upstream[c * half : (c + 1) * half]
        right = left = own
        acc = dot(own, weight_of(me), NT)
        for k in range(1, tp // 2):
            right = lax.ppermute(right, "tp", shift(tp, 1))
            left = lax.ppermute(left, "tp", shift(tp, -1))
            if k == 1:
                firsts.append(right)
            if k == 2:
                seconds.append(right)
            acc = acc + dot(right, weight_of(me - k + tp), NT) + dot(left, weight_of(me + k), NT)
        up = lax.ppermute(right[:BLOCK], "tp", shift(tp, 1))
        down = lax.ppermute(left[BLOCK:], "tp", shift(tp, -1))
        accs.append(acc)
        lasts.append((up, down))

    triangle = (jnp.arange(BLOCK)[:, None] <= jnp.arange(BLOCK)[None, :]).astype(F32)
    cum = jnp.dot(log_decay.reshape(heads * blocks, BLOCK), triangle, precision=lax.Precision.HIGHEST)
    cum = cum.reshape(heads, blocks, BLOCK)
    last = cum[:, :, -1].T
    arow = cum.reshape(heads, tokens)
    aline = arow.T
    bc_then, _ = lax.optimization_barrier((head_bc, firsts[0]))
    sw, dec, sct, wct, spad = prepare(bc_then, arow, aline, states)
    ahead = jnp.exp(jnp.cumsum(last, axis=0) - last)

    own_log, _ = lax.optimization_barrier((jnp.sum(last, axis=0), firsts[1]))
    other_log = from_core(own_log)
    chip_log = own_log + other_log
    y_logs = jnp.stack([chip_log] + from_y(chip_log))
    row_log, _ = lax.optimization_barrier((jnp.sum(y_logs, axis=0), seconds[0]))
    x_logs = jnp.stack([row_log] + from_x(row_log))
    at_y = (py - jnp.arange(4)) % 4
    at_x = (px - jnp.arange(4)) % 4

    def masked(mask, logs):
        return jnp.sum(jnp.where(mask[:, :, None], logs[None], 0.0), axis=1)

    none = jnp.zeros_like(own_log)
    first_core = pc == 0
    after_core = jnp.where(first_core, other_log, none)
    after_y = jnp.sum(jnp.where((at_y > py)[:, None], y_logs, 0.0), axis=0)
    over_y = masked((at_y[None] > py) & (at_y[None] < at_y[:, None]), y_logs)
    over_x = masked((at_x[None] > px) & (at_x[None] < at_x[:, None]), x_logs)
    rows_y = masked(at_y[None] < at_y[:, None], y_logs)
    chips = jnp.stack([jnp.where(first_core, none, other_log), jnp.where(first_core, own_log, none)])
    finals = jnp.concatenate(
        [
            jnp.where(first_core, jnp.ones_like(own_log), none)[None],
            jnp.where((at_y > py)[:, None], jnp.exp(after_core + over_y), 0.0)[1:],
            jnp.where((at_x > px)[:, None], jnp.exp(after_core + after_y + over_x), 0.0)[1:],
        ]
    )
    coefs = jnp.concatenate([jnp.exp(chips), jnp.exp(rows_y), finals])

    skips = skip[None]

    def within(first, count, dy_first, dy, before):
        return inside(
            first, count, dy_first, dy, skips, inner_act, head_bc, sw, aline, dec, sct, spad, before
        )

    source = ((me + tp // 2) % tp).astype(jnp.int32)[None]
    dy0, terms0 = close_chunk(0, source, accs[0], *lasts[0], out_weight, wct, ahead, None)
    grads = within(0, 2, 0, dy0, None)
    lasts[1], coefs, grads = lax.optimization_barrier((lasts[1], coefs, grads))
    dy1, terms1, part = close_chunk(2, source, accs[1], *lasts[1], out_weight, wct, ahead, terms0)

    def by(i):
        return coefs[i][:, None, None]

    part16 = part.astype(BF16)
    other = from_core(part16)
    chip_sum = (by(0) * part + by(1) * other.astype(F32)).astype(BF16)
    ys = from_y(chip_sum)
    dy1, chip_sum = lax.optimization_barrier((dy1, chip_sum))
    grads = within(2, 1, 0, dy1, grads)
    row_sum = by(2) * chip_sum.astype(F32)
    for s in range(3):
        row_sum = row_sum + by(3 + s) * ys[s].astype(F32)
    row_sum = row_sum.astype(BF16)
    xs = from_x(row_sum)
    dy1, row_sum = lax.optimization_barrier((dy1, row_sum))
    dx, dbc, dlog = within(3, 1, 1, dy1, grads)
    return finish(
        coefs[6:], last, [other] + ys + xs, inner_act, head_bc, aline, (terms0, terms1), states, dx, dbc, dlog
    )


def solution(mesh):
    return jax.shard_map(
        per_device,
        mesh=mesh,
        in_specs=(
            P("ctx", "tp"),
            P("tp", None),
            P("ctx", "tp"),
            P("ctx", "tp"),
            P("tp", "ctx"),
            P("ctx", "tp", None, None),
            P("tp"),
        ),
        out_specs=(P("ctx", "tp"), P("ctx", "tp"), P("tp", "ctx")),
        check_vma=False,
    )
```

```python
import jax
import jax.numpy as jnp
from jax import lax
from jax.experimental import pallas as pl
from jax.experimental.pallas import tpu as pltpu
from jax.sharding import PartitionSpec as P

HEAD_DIM = 128
STATE = 64
BLOCK = 256
F32 = jnp.float32
BF16 = jnp.bfloat16
VMEM_LIMIT = 48 << 20


def dot(a, b, dims):
    return lax.dot_general(a, b, (dims, ((), ())), preferred_element_type=F32)


def in_hbm(*arrays):
    return [pltpu.with_memory_space_constraint(a, pltpu.HBM) for a in arrays]


NN = ((1,), (0,))
NT = ((1,), (1,))
TN = ((0,), (0,))


def low_lanes(shape):
    return lax.broadcasted_iota(jnp.int32, shape, len(shape) - 1) < STATE


def log_rows(log):
    high = log.astype(BF16)
    rest = log - high.astype(F32)
    middle = rest.astype(BF16)
    low = (rest - middle.astype(F32)).astype(BF16)
    return high, middle, low


def store_message(ref, sums, logs):
    heads = len(sums)
    for h in range(heads):
        ref[h * STATE : (h + 1) * STATE, :] = sums[h].astype(BF16)
    parts = [log_rows(log) for log in logs]
    rows = [parts[h][k].astype(F32) for k in range(3) for h in range(heads)]
    rows = rows + [jnp.zeros_like(rows[0])] * (16 - 3 * heads)
    ref[heads * STATE :, :] = jnp.concatenate(rows, axis=0).astype(BF16)


def message_sum(ref, h):
    return ref[h * STATE : (h + 1) * STATE, :].astype(F32)


def message_log(ref, heads, h):
    tail = ref[heads * STATE :, :].astype(F32)
    return tail[h : h + 1] + tail[heads + h : heads + h + 1] + tail[2 * heads + h : 2 * heads + h + 1]


def masked_total(terms):
    total = jnp.zeros_like(terms[0][1])
    for condition, value in terms:
        total = total + jnp.where(condition, value, 0.0)
    return total


def combine(kind, place, messages):
    rows, width = messages[0].shape
    heads = (rows - 16) // STATE

    def body(place_ref, *refs):
        got, out_ref = refs[:-1], refs[-1]
        sums, logs = [], []
        for h in range(heads):
            log = [message_log(ref, heads, h) for ref in got]
            if kind == "core":
                first = place_ref[2] == 0
                own = jnp.exp(jnp.where(first, 0.0, log[1]))
                other = jnp.exp(jnp.where(first, log[0], 0.0))
                sums.append(own * message_sum(got[0], h) + other * message_sum(got[1], h))
            else:
                here = [lax.rem(place_ref[1] - s + 4, 4) for s in range(4)]
                total = None
                for s in range(4):
                    ahead = masked_total([(here[t] < here[s], log[t]) for t in range(4) if t != s])
                    term = jnp.exp(ahead) * message_sum(got[s], h)
                    total = term if total is None else total + term
                sums.append(total)
            logs.append(sum(log[1:], log[0]))
        store_message(out_ref, sums, logs)

    return pl.pallas_call(
        body,
        name="combine_" + kind,
        in_specs=[pl.BlockSpec(memory_space=pltpu.SMEM)]
        + [pl.BlockSpec(memory_space=pltpu.VMEM)] * len(messages),
        out_specs=pl.BlockSpec(memory_space=pltpu.VMEM),
        out_shape=jax.ShapeDtypeStruct((rows, width), BF16),
        cost_estimate=pl.CostEstimate(flops=1_000_000, bytes_accessed=500_000, transcendentals=0),
        compiler_params=pltpu.CompilerParams(vmem_limit_bytes=16 << 20),
    )(place, *messages)


def prepare(bc, arow, aline, states):
    tokens, width = bc.shape
    heads = width // HEAD_DIM
    blocks = tokens // BLOCK

    def body(bc_ref, arow_ref, aline_ref, states_ref, sw_ref, dec_ref, sct_ref, wct_ref, spad_ref):
        rows = lax.broadcasted_iota(jnp.int32, (BLOCK, BLOCK), 0)
        cols = lax.broadcasted_iota(jnp.int32, (BLOCK, BLOCK), 1)
        low = low_lanes((BLOCK, HEAD_DIM))
        for h in range(heads):
            lanes = slice(h * HEAD_DIM, (h + 1) * HEAD_DIM)
            gap = aline_ref[:, h : h + 1] - arow_ref[h : h + 1, :]
            dec_ref[0, h] = jnp.where(rows >= cols, jnp.exp(jnp.minimum(gap, 0.0)), 0.0).astype(BF16)
            bc = bc_ref[:, lanes].astype(F32)
            swapped = pltpu.roll(bc, STATE, 1)
            sw_ref[:, lanes] = swapped.astype(BF16)
            c_low = jnp.where(low, swapped, 0.0)
            b_low = jnp.where(low, bc, 0.0)
            scores = dot(b_low.astype(BF16), c_low.astype(BF16), NT)
            back = jnp.where(cols >= rows, jnp.exp(jnp.minimum(-gap, 0.0)), 0.0)
            sct_ref[0, h] = (scores * back).astype(BF16)
            weighted = c_low * jnp.exp(aline_ref[:, h : h + 1])
            wct_ref[0, h] = weighted.T[:STATE, :].astype(BF16)
            state = states_ref[0, h].astype(BF16)
            spad_ref[0, h] = jnp.concatenate([jnp.zeros_like(state), state], axis=0)

    wide = pl.BlockSpec((BLOCK, width), lambda b: (b, 0))

    def block4(*dims):
        return pl.BlockSpec((1, heads) + dims, lambda b: (b, 0, 0, 0))

    return pl.pallas_call(
        body,
        name="prepare",
        grid=(blocks,),
        in_specs=[
            wide,
            pl.BlockSpec((heads, BLOCK), lambda b: (0, b)),
            pl.BlockSpec((BLOCK, heads), lambda b: (b, 0)),
            block4(STATE, HEAD_DIM),
        ],
        out_specs=[
            wide,
            block4(BLOCK, BLOCK),
            block4(BLOCK, BLOCK),
            block4(STATE, BLOCK),
            block4(HEAD_DIM, HEAD_DIM),
        ],
        out_shape=[
            pltpu.HBM((tokens, width), BF16),
            pltpu.HBM((blocks, heads, BLOCK, BLOCK), BF16),
            pltpu.HBM((blocks, heads, BLOCK, BLOCK), BF16),
            pltpu.HBM((blocks, heads, STATE, BLOCK), BF16),
            pltpu.HBM((blocks, heads, HEAD_DIM, HEAD_DIM), BF16),
        ],
        cost_estimate=pl.CostEstimate(flops=4_000_000_000, bytes_accessed=9_000_000, transcendentals=0),
        compiler_params=pltpu.CompilerParams(vmem_limit_bytes=VMEM_LIMIT),
    )(bc, arow, aline, states)


def close_chunk(first, source, acc, up, down, weight, wct, scale, earlier):
    tokens, width = acc.shape
    heads = width // HEAD_DIM
    last = earlier is not None

    def body(source_ref, *refs):
        scale_ref, acc_ref, up_ref, down_ref, weight_ref, wct_ref = refs[:6]
        if last:
            earlier_ref, dy_ref, terms_ref, part_ref = refs[6:]
        else:
            dy_ref, terms_ref = refs[6:]
        sums = [jnp.zeros((STATE, HEAD_DIM), F32) for _ in range(heads)]
        if last:
            for b in range(2):
                for h in range(heads):
                    sums[h] = sums[h] + scale_ref[b, h] * earlier_ref[b, h]
        for b, piece in enumerate((up_ref, down_ref)):
            rows = slice(b * BLOCK, (b + 1) * BLOCK)
            dy = (acc_ref[rows, :] + dot(piece[...], weight_ref[...], NT)).astype(BF16)
            dy_ref[rows, :] = dy
            for h in range(heads):
                term = dot(wct_ref[b, h], dy[:, h * HEAD_DIM : (h + 1) * HEAD_DIM], NN)
                terms_ref[b, h] = term
                if last:
                    sums[h] = sums[h] + scale_ref[b + first, h] * term
        if last:
            store_message(
                part_ref, sums, [jnp.full((1, HEAD_DIM), scale_ref[4, h], F32) for h in range(heads)]
            )

    def whole(*dims):
        return pl.BlockSpec(dims, lambda i, source: (0,) * len(dims))

    terms_shape = (2, heads, STATE, HEAD_DIM)
    out_shape = [pltpu.HBM((tokens, width), BF16), pltpu.HBM(terms_shape, F32)]
    out_specs = [whole(tokens, width), whole(*terms_shape)]
    in_specs = [
        pl.BlockSpec(memory_space=pltpu.SMEM),
        whole(tokens, width),
        whole(*up.shape),
        whole(*down.shape),
        pl.BlockSpec((width, up.shape[1]), lambda i, source: (0, source[0])),
        pl.BlockSpec((2, heads, STATE, BLOCK), lambda i, source: (first // 2, 0, 0, 0)),
    ]
    operands = [scale, acc, up, down, weight, wct]
    if last:
        out_shape.append(jax.ShapeDtypeStruct((heads * STATE + 16, HEAD_DIM), BF16))
        out_specs.append(whole(heads * STATE + 16, HEAD_DIM))
        in_specs.append(whole(*terms_shape))
        operands.extend(in_hbm(earlier))
    return pl.pallas_call(
        body,
        name="close_chunk",
        grid_spec=pltpu.PrefetchScalarGridSpec(
            num_scalar_prefetch=1, grid=(1,), in_specs=in_specs, out_specs=out_specs
        ),
        out_shape=out_shape,
        cost_estimate=pl.CostEstimate(flops=600_000_000, bytes_accessed=4_000_000, transcendentals=0),
        compiler_params=pltpu.CompilerParams(vmem_limit_bytes=VMEM_LIMIT),
    )(source, *operands)


def inside(first, count, dy_first, dy, skip, x, bc, sw, aline, dec, sct, spad, before):
    tokens, width = x.shape
    heads = width // HEAD_DIM
    group = heads // 2

    def body(skip_ref, dy_ref, x_ref, bc_ref, sw_ref, aline_ref, dec_ref, sct_ref, spad_ref, *rest):
        dx_ref, dbc_ref, dlog_ref = rest[-3:]
        base = pl.program_id(1) * group
        rows = lax.broadcasted_iota(jnp.int32, (BLOCK, BLOCK), 0)
        cols = lax.broadcasted_iota(jnp.int32, (BLOCK, BLOCK), 1)
        low = low_lanes((BLOCK, HEAD_DIM))
        for h in range(group):
            lanes = slice(h * HEAD_DIM, (h + 1) * HEAD_DIM)
            dy_h = dy_ref[:, lanes]
            x_h = x_ref[:, lanes]
            bc_h = bc_ref[:, lanes]
            sw_h = sw_ref[:, lanes]
            zero = jnp.zeros_like(sw_h)
            gaps = dot(dy_h, x_h, NT)
            mixed = (gaps * dec_ref[0, h].astype(F32)).astype(BF16)
            dx_ref[:, lanes] = dot(sct_ref[0, h], dy_h, NN) + skip_ref[0, base + h] * dy_h.astype(F32)
            grad = dot(mixed, jnp.where(low, zero, sw_h), NN)
            grad = grad + dot(mixed, jnp.where(low, sw_h, zero), TN)
            grad = grad + jnp.exp(aline_ref[0][:, h : h + 1]) * dot(dy_h, spad_ref[0, h], NT)
            dbc_ref[:, lanes] = grad
            signed = grad * bc_h.astype(F32)
            moved = jnp.sum(jnp.where(low, -signed, signed), axis=1, keepdims=True)
            dlog_ref[h] = jnp.sum(jnp.where(rows >= cols, moved, 0.0), axis=0, keepdims=True)

    wide = pl.BlockSpec((BLOCK, group * HEAD_DIM), lambda b, g: (b + first, g))
    square = pl.BlockSpec((1, group, BLOCK, BLOCK), lambda b, g: (b + first, g, 0, 0))
    in_specs = [
        pl.BlockSpec(memory_space=pltpu.SMEM),
        pl.BlockSpec((BLOCK, group * HEAD_DIM), lambda b, g: (b + dy_first, g)),
        wide,
        wide,
        wide,
        pl.BlockSpec((1, BLOCK, group), lambda b, g: (g, b + first, 0)),
        square,
        square,
        pl.BlockSpec((1, group, HEAD_DIM, HEAD_DIM), lambda b, g: (b + first, g, 0, 0)),
    ]
    dy, x, bc, sw, dec, sct, spad = in_hbm(dy, x, bc, sw, dec, sct, spad)
    operands = [skip, dy, x, bc, sw, aline, dec, sct, spad]
    aliases = {}
    if before is not None:
        for place, array in enumerate(in_hbm(*before)):
            aliases[len(operands)] = place
            operands.append(array)
            in_specs.append(pl.BlockSpec(memory_space=pl.ANY))
    return pl.pallas_call(
        body,
        name="inside",
        grid=(count, 2),
        in_specs=in_specs,
        out_specs=[wide, wide, pl.BlockSpec((group, 1, BLOCK), lambda b, g: (g, 0, b + first))],
        out_shape=[
            pltpu.HBM((tokens, width), F32),
            pltpu.HBM((tokens, width), F32),
            pltpu.HBM((heads, 1, tokens), F32),
        ],
        input_output_aliases=aliases,
        cost_estimate=pl.CostEstimate(
            flops=1_000_000_000 * count, bytes_accessed=3_500_000 * count, transcendentals=0
        ),
        compiler_params=pltpu.CompilerParams(vmem_limit_bytes=VMEM_LIMIT),
    )(*operands)


def finish(place, a_last, received, x, bc, aline, terms, states, dx, dbc, dlog):
    tokens, width = x.shape
    heads = width // HEAD_DIM
    blocks = tokens // BLOCK
    count = len(received)

    def body(place_ref, last_ref, *refs):
        got = refs[:count]
        (x_ref, bc_ref, aline_ref, terms0_ref, terms1_ref, states_ref, dx_ref, dbc_ref, dlog_ref, out_ref,
         outbc_ref, outlog_ref, carry_ref) = refs[count:]
        step = pl.program_id(0)
        b = blocks - 1 - step

        @pl.when(step == 0)
        def _():
            own, other, ys, xs = got[0], got[1], got[2:6], got[6:10]
            first = place_ref[2] == 0
            at_y = [lax.rem(place_ref[1] - s + 4, 4) for s in range(4)]
            at_x = [lax.rem(place_ref[0] - s + 4, 4) for s in range(4)]
            for h in range(heads):
                y_logs = [message_log(ref, heads, h) for ref in ys]
                x_logs = [message_log(ref, heads, h) for ref in xs]
                after_core = jnp.where(first, message_log(other, heads, h), 0.0)
                after_y = after_core + masked_total([(at_y[t] > at_y[0], y_logs[t]) for t in (1, 2, 3)])
                total = jnp.where(first, message_sum(other, h), 0.0)
                for places, logs, items, after in ((at_y, y_logs, ys, after_core), (at_x, x_logs, xs, after_y)):
                    for s in (1, 2, 3):
                        between = masked_total(
                            [
                                ((places[t] > places[0]) & (places[t] < places[s]), logs[t])
                                for t in (1, 2, 3)
                                if t != s
                            ]
                        )
                        factor = jnp.where(places[s] > places[0], jnp.exp(after + between), 0.0)
                        total = total + factor * message_sum(items[s], h)
                carry_ref[h] = total

        rows = lax.broadcasted_iota(jnp.int32, (BLOCK, BLOCK), 0)
        cols = lax.broadcasted_iota(jnp.int32, (BLOCK, BLOCK), 1)
        late = step < blocks // 2
        for h in range(heads):
            lanes = slice(h * HEAD_DIM, (h + 1) * HEAD_DIM)
            carry = carry_ref[h]
            carry16 = carry.astype(BF16)
            last = last_ref[b, h]
            tail = jnp.exp(last - aline_ref[:, h : h + 1])
            bc_h = bc_ref[:, lanes].astype(F32)
            weighted = (bc_h * tail).astype(BF16)[:, :STATE]
            out_ref[:, lanes] = (dx_ref[:, lanes] + dot(weighted, carry16, NN)).astype(BF16)
            padded = jnp.concatenate([carry16, jnp.zeros_like(carry16)], axis=0)
            extra = tail * dot(x_ref[:, lanes], padded, NT)
            outbc_ref[:, lanes] = dbc_ref[:, lanes] + extra
            moved = jnp.sum(extra * bc_h, axis=1, keepdims=True)
            ends = jnp.exp(jnp.full((1, HEAD_DIM), last, F32))
            whole = jnp.sum(jnp.sum(states_ref[0, h] * carry, axis=0, keepdims=True) * ends)
            outlog_ref[h : h + 1, :] = (
                dlog_ref[h] + jnp.sum(jnp.where(rows < cols, moved, 0.0), axis=0, keepdims=True) + whole
            )
            carry_ref[h] = ends * carry + jnp.where(late, terms1_ref[0, h], terms0_ref[0, h])

    x, bc, states, dx, dbc, dlog = in_hbm(x, bc, states, dx, dbc, dlog)
    terms = in_hbm(*terms)
    wide = pl.BlockSpec((BLOCK, width), lambda i: (blocks - 1 - i, 0))
    smem = pl.BlockSpec(memory_space=pltpu.SMEM)
    state_block = (1, heads, STATE, HEAD_DIM)
    half = blocks // 2
    return pl.pallas_call(
        body,
        name="finish",
        grid=(blocks,),
        in_specs=[smem, smem]
        + [pl.BlockSpec(message.shape, lambda i: (0, 0)) for message in received]
        + [
            wide,
            wide,
            pl.BlockSpec((BLOCK, heads), lambda i: (blocks - 1 - i, 0)),
            pl.BlockSpec(state_block, lambda i: (jnp.clip(blocks - 1 - i, 0, half - 1), 0, 0, 0)),
            pl.BlockSpec(state_block, lambda i: (jnp.clip(half - 1 - i, 0, half - 1), 0, 0, 0)),
            pl.BlockSpec(state_block, lambda i: (blocks - 1 - i, 0, 0, 0)),
            wide,
            wide,
            pl.BlockSpec((heads, 1, BLOCK), lambda i: (0, 0, blocks - 1 - i)),
        ],
        out_specs=[wide, wide, pl.BlockSpec((heads, BLOCK), lambda i: (0, blocks - 1 - i))],
        out_shape=[
            jax.ShapeDtypeStruct((tokens, width), BF16),
            jax.ShapeDtypeStruct((tokens, width), F32),
            jax.ShapeDtypeStruct((heads, tokens), F32),
        ],
        scratch_shapes=[pltpu.VMEM((heads, STATE, HEAD_DIM), F32)],
        cost_estimate=pl.CostEstimate(flops=600_000_000, bytes_accessed=11_000_000, transcendentals=0),
        compiler_params=pltpu.CompilerParams(vmem_limit_bytes=VMEM_LIMIT),
    )(place, a_last, *received, x, bc, aline, terms[0], terms[1], states, dx, dbc, dlog)


def shift(count, by):
    return [(i, (i + by) % count) for i in range(count)]


def per_device(upstream, out_weight, inner_act, head_bc, log_decay, states, skip):
    tokens, width = inner_act.shape
    heads = log_decay.shape[0]
    blocks = tokens // BLOCK
    tp = lax.axis_size("tp")
    me = lax.axis_index("tp")
    ctx = lax.axis_index("ctx")
    feats = upstream.shape[1]
    px, py, pc = ctx // 8, (ctx // 2) % 4, ctx % 2

    places = [(x, y, c) for x in range(4) for y in range(4) for c in range(2)]

    def perm(dx, dy, dc):
        return [(x * 8 + y * 2 + c, ((x + dx) % 4) * 8 + ((y + dy) % 4) * 2 + (c ^ dc)) for x, y, c in places]

    def from_core(a):
        return lax.ppermute(a, "ctx", perm(0, 0, 1))

    def from_y(a):
        return [lax.ppermute(a, "ctx", perm(0, s, 0)) for s in (1, 2, 3)]

    def from_x(a):
        return [lax.ppermute(a, "ctx", perm(s, 0, 0)) for s in (1, 2, 3)]

    def weight_of(source):
        return lax.dynamic_slice_in_dim(out_weight, (source % tp) * feats, feats, 1)

    half = tokens // 2
    accs, lasts, firsts = [], [], []
    for c in range(2):
        own = upstream[c * half : (c + 1) * half]
        right = left = own
        acc = dot(own, weight_of(me), NT)
        for k in range(1, tp // 2):
            right = lax.ppermute(right, "tp", shift(tp, 1))
            left = lax.ppermute(left, "tp", shift(tp, -1))
            if k == 1:
                firsts.append(right)
            acc = acc + dot(right, weight_of(me - k + tp), NT) + dot(left, weight_of(me + k), NT)
        up = lax.ppermute(right[:BLOCK], "tp", shift(tp, 1))
        down = lax.ppermute(left[BLOCK:], "tp", shift(tp, -1))
        accs.append(acc)
        lasts.append((up, down))

    triangle = (jnp.arange(BLOCK)[:, None] <= jnp.arange(BLOCK)[None, :]).astype(F32)
    cum = jnp.dot(log_decay.reshape(heads * blocks, BLOCK), triangle, precision=lax.Precision.HIGHEST)
    cum = cum.reshape(heads, blocks, BLOCK)
    last = cum[:, :, -1].T
    arow = cum.reshape(heads, tokens)
    aline = arow.T
    bc_then, _ = lax.optimization_barrier((head_bc, firsts[0]))
    sw, dec, sct, wct, spad = prepare(bc_then, arow, aline, states)
    upto = jnp.cumsum(last, axis=0)
    scale = jnp.concatenate([jnp.exp(upto - last), upto[blocks - 1 :]])
    place = jnp.stack([px, py, pc]).astype(jnp.int32)

    skips = skip[None]
    aline2 = jnp.stack([aline[:, : heads // 2], aline[:, heads // 2 :]])

    def within(first, count, dy_first, dy, before):
        return inside(
            first, count, dy_first, dy, skips, inner_act, head_bc, sw, aline2, dec, sct, spad, before
        )

    source = ((me + tp // 2) % tp).astype(jnp.int32)[None]
    dy0, terms0 = close_chunk(0, source, accs[0], *lasts[0], out_weight, wct, scale, None)
    dy1, terms1, part = close_chunk(2, source, accs[1], *lasts[1], out_weight, wct, scale, terms0)

    other = from_core(part)
    chip = combine("core", place, [part, other])
    ys = [chip] + from_y(chip)
    dy0, ys[0] = lax.optimization_barrier((dy0, ys[0]))
    grads = within(0, 2, 0, dy0, None)
    row = combine("row", place, ys)
    xs = [row] + from_x(row)
    dy1, xs[0] = lax.optimization_barrier((dy1, xs[0]))
    dx, dbc, dlog = within(2, 2, 0, dy1, grads)
    return finish(
        place, last, [part, other] + ys + xs, inner_act, head_bc, aline, (terms0, terms1), states, dx, dbc, dlog
    )


def solution(mesh):
    return jax.shard_map(
        per_device,
        mesh=mesh,
        in_specs=(
            P("ctx", "tp"),
            P("tp", None),
            P("ctx", "tp"),
            P("ctx", "tp"),
            P("tp", "ctx"),
            P("ctx", "tp", None, None),
            P("tp"),
        ),
        out_specs=(P("ctx", "tp"), P("ctx", "tp"), P("tp", "ctx")),
        check_vma=False,
    )
```

```python
import jax
import jax.numpy as jnp
from jax import lax
from jax.experimental import pallas as pl
from jax.experimental.pallas import tpu as pltpu
from jax.sharding import PartitionSpec as P

HEAD_DIM = 128
STATE = 64
BLOCK = 256
F32 = jnp.float32
BF16 = jnp.bfloat16
VMEM_LIMIT = 40 << 20


def dot(a, b, dims):
    return lax.dot_general(a, b, (dims, ((), ())), preferred_element_type=F32)


def in_hbm(*arrays):
    return [pltpu.with_memory_space_constraint(a, pltpu.HBM) for a in arrays]


NN = ((1,), (0,))
NT = ((1,), (1,))
TN = ((0,), (0,))


def low_lanes(shape):
    return lax.broadcasted_iota(jnp.int32, shape, len(shape) - 1) < STATE


def log_rows(log):
    high = log.astype(BF16)
    rest = log - high.astype(F32)
    middle = rest.astype(BF16)
    low = (rest - middle.astype(F32)).astype(BF16)
    return high, middle, low


def store_message(ref, sums, logs):
    heads = len(sums)
    for h in range(heads):
        ref[h * STATE : (h + 1) * STATE, :] = sums[h].astype(BF16)
    parts = [log_rows(log) for log in logs]
    rows = [parts[h][k].astype(F32) for k in range(3) for h in range(heads)]
    rows = rows + [jnp.zeros_like(rows[0])] * (16 - 3 * heads)
    ref[heads * STATE :, :] = jnp.concatenate(rows, axis=0).astype(BF16)


def message_sum(ref, h):
    return ref[h * STATE : (h + 1) * STATE, :].astype(F32)


def message_log(ref, heads, h):
    tail = ref[heads * STATE :, :].astype(F32)
    return tail[h : h + 1] + tail[heads + h : heads + h + 1] + tail[2 * heads + h : 2 * heads + h + 1]


def masked_total(terms):
    total = jnp.zeros_like(terms[0][1])
    for condition, value in terms:
        total = total + jnp.where(condition, value, 0.0)
    return total


def combine(kind, place, messages):
    rows, width = messages[0].shape
    heads = (rows - 16) // STATE

    def body(place_ref, *refs):
        got, out_ref = refs[:-1], refs[-1]
        sums, logs = [], []
        for h in range(heads):
            log = [message_log(ref, heads, h) for ref in got]
            if kind == "core":
                first = place_ref[2] == 0
                own = jnp.exp(jnp.where(first, 0.0, log[1]))
                other = jnp.exp(jnp.where(first, log[0], 0.0))
                sums.append(own * message_sum(got[0], h) + other * message_sum(got[1], h))
            else:
                here = [lax.rem(place_ref[1] - s + 4, 4) for s in range(4)]
                total = None
                for s in range(4):
                    ahead = masked_total([(here[t] < here[s], log[t]) for t in range(4) if t != s])
                    term = jnp.exp(ahead) * message_sum(got[s], h)
                    total = term if total is None else total + term
                sums.append(total)
            logs.append(sum(log[1:], log[0]))
        store_message(out_ref, sums, logs)

    return pl.pallas_call(
        body,
        name="combine_" + kind,
        in_specs=[pl.BlockSpec(memory_space=pltpu.SMEM)]
        + [pl.BlockSpec(memory_space=pltpu.VMEM)] * len(messages),
        out_specs=pl.BlockSpec(memory_space=pltpu.VMEM),
        out_shape=jax.ShapeDtypeStruct((rows, width), BF16),
        cost_estimate=pl.CostEstimate(flops=1_000_000, bytes_accessed=500_000, transcendentals=0),
        compiler_params=pltpu.CompilerParams(vmem_limit_bytes=16 << 20),
    )(place, *messages)


def prepare(bc, arow, aline, states):
    tokens, width = bc.shape
    heads = width // HEAD_DIM
    blocks = tokens // BLOCK

    def body(bc_ref, arow_ref, aline_ref, states_ref, sw_ref, dec_ref, sct_ref, wct_ref, spad_ref):
        rows = lax.broadcasted_iota(jnp.int32, (BLOCK, BLOCK), 0)
        cols = lax.broadcasted_iota(jnp.int32, (BLOCK, BLOCK), 1)
        low = low_lanes((BLOCK, HEAD_DIM))
        for h in range(heads):
            lanes = slice(h * HEAD_DIM, (h + 1) * HEAD_DIM)
            gap = aline_ref[:, h : h + 1] - arow_ref[h : h + 1, :]
            dec_ref[0, h] = jnp.where(rows >= cols, jnp.exp(jnp.minimum(gap, 0.0)), 0.0).astype(BF16)
            bc = bc_ref[:, lanes].astype(F32)
            swapped = pltpu.roll(bc, STATE, 1)
            sw_ref[:, lanes] = swapped.astype(BF16)
            c_low = jnp.where(low, swapped, 0.0)
            b_low = jnp.where(low, bc, 0.0)
            scores = dot(b_low.astype(BF16), c_low.astype(BF16), NT)
            back = jnp.where(cols >= rows, jnp.exp(jnp.minimum(-gap, 0.0)), 0.0)
            sct_ref[0, h] = (scores * back).astype(BF16)
            weighted = c_low * jnp.exp(aline_ref[:, h : h + 1])
            wct_ref[0, h] = weighted.T[:STATE, :].astype(BF16)
            state = states_ref[0, h].astype(BF16)
            spad_ref[0, h] = jnp.concatenate([jnp.zeros_like(state), state], axis=0)

    wide = pl.BlockSpec((BLOCK, width), lambda b: (b, 0))

    def block4(*dims):
        return pl.BlockSpec((1, heads) + dims, lambda b: (b, 0, 0, 0))

    return pl.pallas_call(
        body,
        name="prepare",
        grid=(blocks,),
        in_specs=[
            wide,
            pl.BlockSpec((heads, BLOCK), lambda b: (0, b)),
            pl.BlockSpec((BLOCK, heads), lambda b: (b, 0)),
            block4(STATE, HEAD_DIM),
        ],
        out_specs=[
            wide,
            block4(BLOCK, BLOCK),
            block4(BLOCK, BLOCK),
            block4(STATE, BLOCK),
            block4(HEAD_DIM, HEAD_DIM),
        ],
        out_shape=[
            pltpu.HBM((tokens, width), BF16),
            pltpu.HBM((blocks, heads, BLOCK, BLOCK), BF16),
            pltpu.HBM((blocks, heads, BLOCK, BLOCK), BF16),
            pltpu.HBM((blocks, heads, STATE, BLOCK), BF16),
            pltpu.HBM((blocks, heads, HEAD_DIM, HEAD_DIM), BF16),
        ],
        cost_estimate=pl.CostEstimate(flops=4_000_000_000, bytes_accessed=9_000_000, transcendentals=0),
        compiler_params=pltpu.CompilerParams(vmem_limit_bytes=VMEM_LIMIT),
    )(bc, arow, aline, states)


def resident():
    return pl.BlockSpec(memory_space=pltpu.VMEM)


def close_chunk(first, source, acc, up, down, weight, wct, scale, earlier):
    tokens, width = acc.shape
    heads = width // HEAD_DIM
    feats = up.shape[1]
    last = earlier is not None

    def body(source_ref, scale_ref, acc_ref, up_ref, down_ref, weight_ref, wct_ref, *refs):
        if last:
            earlier_ref, dy_ref, terms_ref, part_ref = refs
        else:
            dy_ref, terms_ref = refs
        weights = weight_ref[:, pl.ds(pl.multiple_of(source_ref[0] * feats, feats), feats)]
        sums = [jnp.zeros((STATE, HEAD_DIM), F32) for _ in range(heads)]
        if last:
            for b in range(2):
                for h in range(heads):
                    sums[h] = sums[h] + scale_ref[b, h] * earlier_ref[b, h]
        for b, piece in enumerate((up_ref, down_ref)):
            rows = slice(b * BLOCK, (b + 1) * BLOCK)
            dy = (acc_ref[rows, :] + dot(piece[...], weights, NT)).astype(BF16)
            dy_ref[rows, :] = dy
            for h in range(heads):
                term = dot(wct_ref[first + b, h], dy[:, h * HEAD_DIM : (h + 1) * HEAD_DIM], NN)
                terms_ref[b, h] = term
                if last:
                    sums[h] = sums[h] + scale_ref[b + first, h] * term
        if last:
            store_message(
                part_ref, sums, [jnp.full((1, HEAD_DIM), scale_ref[4, h], F32) for h in range(heads)]
            )

    smem = pl.BlockSpec(memory_space=pltpu.SMEM)
    out_shape = [
        jax.ShapeDtypeStruct((tokens, width), BF16),
        jax.ShapeDtypeStruct((2, heads, STATE, HEAD_DIM), F32),
    ]
    operands = [source, scale, acc, up, down, weight, wct]
    if last:
        out_shape.append(jax.ShapeDtypeStruct((heads * STATE + 16, HEAD_DIM), BF16))
        operands.append(earlier)
    return pl.pallas_call(
        body,
        name="close_chunk",
        in_specs=[smem, smem] + [resident()] * (len(operands) - 2),
        out_specs=[resident()] * len(out_shape),
        out_shape=out_shape,
        cost_estimate=pl.CostEstimate(flops=600_000_000, bytes_accessed=4_000_000, transcendentals=0),
        compiler_params=pltpu.CompilerParams(vmem_limit_bytes=VMEM_LIMIT),
    )(*operands)


def inside(first, count, dy_first, dy, skip, x, bc, sw, rise, dec, sct, spad):
    width = x.shape[1]
    heads = width // HEAD_DIM

    def body(skip_ref, dy_ref, x_ref, bc_ref, sw_ref, rise_ref, dec_ref, sct_ref, spad_ref, dx_ref, dbc_ref, dlog_ref):
        b = pl.program_id(0)
        here = pl.ds(pl.multiple_of((b + dy_first) * BLOCK, BLOCK), BLOCK)
        there = pl.ds(pl.multiple_of(b * BLOCK, BLOCK), BLOCK)
        rows = lax.broadcasted_iota(jnp.int32, (BLOCK, BLOCK), 0)
        cols = lax.broadcasted_iota(jnp.int32, (BLOCK, BLOCK), 1)
        low = low_lanes((BLOCK, HEAD_DIM))
        for h in range(heads):
            lanes = slice(h * HEAD_DIM, (h + 1) * HEAD_DIM)
            dy_h = dy_ref[here, lanes]
            x_h = x_ref[:, lanes]
            bc_h = bc_ref[:, lanes]
            sw_h = sw_ref[:, lanes]
            zero = jnp.zeros_like(sw_h)
            gaps = dot(dy_h, x_h, NT)
            mixed = (gaps * dec_ref[0, h].astype(F32)).astype(BF16)
            dx_ref[there, lanes] = dot(sct_ref[0, h], dy_h, NN) + skip_ref[0, h] * dy_h.astype(F32)
            grad = dot(mixed, jnp.where(low, zero, sw_h), NN)
            grad = grad + dot(mixed, jnp.where(low, sw_h, zero), TN)
            grad = grad + rise_ref[:, h : h + 1] * dot(dy_h, spad_ref[0, h], NT)
            dbc_ref[there, lanes] = grad
            signed = grad * bc_h.astype(F32)
            moved = jnp.sum(jnp.where(low, -signed, signed), axis=1, keepdims=True)
            dlog_ref[b, h : h + 1, :] = jnp.sum(jnp.where(rows >= cols, moved, 0.0), axis=0, keepdims=True)

    wide = pl.BlockSpec((BLOCK, width), lambda b: (b + first, 0))
    square = pl.BlockSpec((1, heads, BLOCK, BLOCK), lambda b: (b + first, 0, 0, 0))
    x, bc, sw, dec, sct, spad = in_hbm(x, bc, sw, dec, sct, spad)
    return pl.pallas_call(
        body,
        name="inside",
        grid=(count,),
        in_specs=[
            pl.BlockSpec(memory_space=pltpu.SMEM),
            resident(),
            wide,
            wide,
            wide,
            pl.BlockSpec((BLOCK, heads), lambda b: (b + first, 0)),
            square,
            square,
            pl.BlockSpec((1, heads, HEAD_DIM, HEAD_DIM), lambda b: (b + first, 0, 0, 0)),
        ],
        out_specs=[resident()] * 3,
        out_shape=[
            jax.ShapeDtypeStruct((count * BLOCK, width), F32),
            jax.ShapeDtypeStruct((count * BLOCK, width), F32),
            jax.ShapeDtypeStruct((count, heads, BLOCK), F32),
        ],
        cost_estimate=pl.CostEstimate(
            flops=1_000_000_000 * count, bytes_accessed=3_500_000 * count, transcendentals=0
        ),
        compiler_params=pltpu.CompilerParams(vmem_limit_bytes=VMEM_LIMIT),
    )(skip, dy, x, bc, sw, rise, dec, sct, spad)


def finish(place, a_last, received, x, bc, fall, terms, states, grads):
    tokens, width = x.shape
    heads = width // HEAD_DIM
    blocks = tokens // BLOCK
    count = len(received)
    starts = [first for first, *_ in grads] + [blocks]
    flat = [array for _, *arrays in grads for array in arrays]

    def body(place_ref, last_ref, *refs):
        got = refs[:count]
        x_ref, bc_ref, fall_ref, terms0_ref, terms1_ref, states_ref = refs[count : count + 6]
        grad_refs = refs[count + 6 : -4]
        out_ref, outbc_ref, outlog_ref, carry_ref = refs[-4:]
        step = pl.program_id(0)
        b = blocks - 1 - step

        @pl.when(step == 0)
        def _():
            own, other, ys, xs = got[0], got[1], got[2:6], got[6:10]
            first = place_ref[2] == 0
            at_y = [lax.rem(place_ref[1] - s + 4, 4) for s in range(4)]
            at_x = [lax.rem(place_ref[0] - s + 4, 4) for s in range(4)]
            for h in range(heads):
                y_logs = [message_log(ref, heads, h) for ref in ys]
                x_logs = [message_log(ref, heads, h) for ref in xs]
                after_core = jnp.where(first, message_log(other, heads, h), 0.0)
                after_y = after_core + masked_total([(at_y[t] > at_y[0], y_logs[t]) for t in (1, 2, 3)])
                total = jnp.where(first, message_sum(other, h), 0.0)
                for places, logs, items, after in ((at_y, y_logs, ys, after_core), (at_x, x_logs, xs, after_y)):
                    for s in (1, 2, 3):
                        between = masked_total(
                            [
                                ((places[t] > places[0]) & (places[t] < places[s]), logs[t])
                                for t in (1, 2, 3)
                                if t != s
                            ]
                        )
                        factor = jnp.where(places[s] > places[0], jnp.exp(after + between), 0.0)
                        total = total + factor * message_sum(items[s], h)
                carry_ref[h] = total

        rows = lax.broadcasted_iota(jnp.int32, (BLOCK, BLOCK), 0)
        cols = lax.broadcasted_iota(jnp.int32, (BLOCK, BLOCK), 1)

        def run(first, dx_ref, dbc_ref, dlog_ref):
            here = pl.ds(pl.multiple_of((b - first) * BLOCK, BLOCK), BLOCK)
            terms_ref = terms0_ref if first < 2 else terms1_ref
            for h in range(heads):
                lanes = slice(h * HEAD_DIM, (h + 1) * HEAD_DIM)
                carry = carry_ref[h]
                carry16 = carry.astype(BF16)
                tail = fall_ref[:, h : h + 1]
                bc_h = bc_ref[:, lanes].astype(F32)
                weighted = (bc_h * tail).astype(BF16)[:, :STATE]
                out_ref[:, lanes] = (dx_ref[here, lanes] + dot(weighted, carry16, NN)).astype(BF16)
                padded = jnp.concatenate([carry16, jnp.zeros_like(carry16)], axis=0)
                extra = tail * dot(x_ref[:, lanes], padded, NT)
                outbc_ref[:, lanes] = dbc_ref[here, lanes] + extra
                moved = jnp.sum(extra * bc_h, axis=1, keepdims=True)
                ends = jnp.exp(jnp.full((1, HEAD_DIM), last_ref[b, h], F32))
                whole = jnp.sum(jnp.sum(states_ref[0, h] * carry, axis=0, keepdims=True) * ends)
                outlog_ref[h : h + 1, :] = (
                    dlog_ref[b - first, h : h + 1, :]
                    + jnp.sum(jnp.where(rows < cols, moved, 0.0), axis=0, keepdims=True)
                    + whole
                )
                carry_ref[h] = ends * carry + terms_ref[b % 2, h]

        for k in range(len(grads)):

            @pl.when((b >= starts[k]) & (b < starts[k + 1]))
            def _(k=k):
                run(starts[k], *grad_refs[3 * k : 3 * k + 3])

    x, bc, states = in_hbm(x, bc, states)
    wide = pl.BlockSpec((BLOCK, width), lambda i: (blocks - 1 - i, 0))
    smem = pl.BlockSpec(memory_space=pltpu.SMEM)
    return pl.pallas_call(
        body,
        name="finish",
        grid=(blocks,),
        in_specs=[smem, smem]
        + [resident()] * count
        + [
            wide,
            wide,
            pl.BlockSpec((BLOCK, heads), lambda i: (blocks - 1 - i, 0)),
            resident(),
            resident(),
            pl.BlockSpec((1, heads, STATE, HEAD_DIM), lambda i: (blocks - 1 - i, 0, 0, 0)),
        ]
        + [resident()] * len(flat),
        out_specs=[wide, wide, pl.BlockSpec((heads, BLOCK), lambda i: (0, blocks - 1 - i))],
        out_shape=[
            jax.ShapeDtypeStruct((tokens, width), BF16),
            jax.ShapeDtypeStruct((tokens, width), F32),
            jax.ShapeDtypeStruct((heads, tokens), F32),
        ],
        scratch_shapes=[pltpu.VMEM((heads, STATE, HEAD_DIM), F32)],
        cost_estimate=pl.CostEstimate(flops=600_000_000, bytes_accessed=11_000_000, transcendentals=0),
        compiler_params=pltpu.CompilerParams(vmem_limit_bytes=VMEM_LIMIT),
    )(place, a_last, *received, x, bc, fall, terms[0], terms[1], states, *flat)


def shift(count, by):
    return [(i, (i + by) % count) for i in range(count)]


def per_device(upstream, out_weight, inner_act, head_bc, log_decay, states, skip):
    tokens, width = inner_act.shape
    heads = log_decay.shape[0]
    blocks = tokens // BLOCK
    tp = lax.axis_size("tp")
    me = lax.axis_index("tp")
    ctx = lax.axis_index("ctx")
    feats = upstream.shape[1]
    px, py, pc = ctx // 8, (ctx // 2) % 4, ctx % 2

    places = [(x, y, c) for x in range(4) for y in range(4) for c in range(2)]

    def perm(dx, dy, dc):
        return [(x * 8 + y * 2 + c, ((x + dx) % 4) * 8 + ((y + dy) % 4) * 2 + (c ^ dc)) for x, y, c in places]

    def from_core(a):
        return lax.ppermute(a, "ctx", perm(0, 0, 1))

    def from_y(a):
        return [lax.ppermute(a, "ctx", perm(0, s, 0)) for s in (1, 2, 3)]

    def from_x(a):
        return [lax.ppermute(a, "ctx", perm(s, 0, 0)) for s in (1, 2, 3)]

    def weight_of(source):
        return lax.dynamic_slice_in_dim(out_weight, (source % tp) * feats, feats, 1)

    half = tokens // 2
    accs, lasts, firsts = [], [], []
    for c in range(2):
        own = upstream[c * half : (c + 1) * half]
        right = left = own
        acc = dot(own, weight_of(me), NT)
        for k in range(1, tp // 2):
            right = lax.ppermute(right, "tp", shift(tp, 1))
            left = lax.ppermute(left, "tp", shift(tp, -1))
            if k == 1:
                firsts.append(right)
            acc = acc + dot(right, weight_of(me - k + tp), NT) + dot(left, weight_of(me + k), NT)
        up = lax.ppermute(right[:BLOCK], "tp", shift(tp, 1))
        down = lax.ppermute(left[BLOCK:], "tp", shift(tp, -1))
        accs.append(acc)
        lasts.append((up, down))

    triangle = (jnp.arange(BLOCK)[:, None] <= jnp.arange(BLOCK)[None, :]).astype(F32)
    cum = jnp.dot(log_decay.reshape(heads * blocks, BLOCK), triangle, precision=lax.Precision.HIGHEST)
    cum = cum.reshape(heads, blocks, BLOCK)
    last = cum[:, :, -1].T
    arow = cum.reshape(heads, tokens)
    aline = arow.T
    bc_then, _ = lax.optimization_barrier((head_bc, firsts[0]))
    sw, dec, sct, wct, spad = prepare(bc_then, arow, aline, states)
    upto = jnp.cumsum(last, axis=0)
    scale = jnp.concatenate([jnp.exp(upto - last), upto[blocks - 1 :]])
    place = jnp.stack([px, py, pc]).astype(jnp.int32)

    skips = skip[None]
    rise = jnp.exp(aline)
    fall = jnp.exp((cum[:, :, -1:] - cum).reshape(heads, tokens).T)

    def within(first, count, dy_first, dy):
        grads = inside(first, count, dy_first, dy, skips, inner_act, head_bc, sw, rise, dec, sct, spad)
        return (first, *grads)

    source = ((me + tp // 2) % tp).astype(jnp.int32)[None]
    dy0, terms0 = close_chunk(0, source, accs[0], *lasts[0], out_weight, wct, scale, None)
    grads0 = within(0, 1, 0, dy0)
    terms0, last_grad, fall = lax.optimization_barrier((terms0, grads0[3], fall))
    grads0 = grads0[:3] + (last_grad,)
    dy1, terms1, part = close_chunk(2, source, accs[1], *lasts[1], out_weight, wct, scale, terms0)
    other = from_core(part)
    chip = combine("core", place, [part, other])
    ys = [chip] + from_y(chip)
    dy0, ys[0] = lax.optimization_barrier((dy0, ys[0]))
    grads1 = within(1, 1, 1, dy0)
    row = combine("row", place, ys)
    xs = [row] + from_x(row)
    dy1, xs[0] = lax.optimization_barrier((dy1, xs[0]))
    grads2 = within(2, 2, 0, dy1)
    return finish(
        place, last, [part, other] + ys + xs, inner_act, head_bc, fall, (terms0, terms1), states,
        [grads0, grads1, grads2],
    )


def solution(mesh):
    return jax.shard_map(
        per_device,
        mesh=mesh,
        in_specs=(
            P("ctx", "tp"),
            P("tp", None),
            P("ctx", "tp"),
            P("ctx", "tp"),
            P("tp", "ctx"),
            P("ctx", "tp", None, None),
            P("tp"),
        ),
        out_specs=(P("ctx", "tp"), P("ctx", "tp"), P("tp", "ctx")),
        check_vma=False,
    )
```

```python
import jax
import jax.numpy as jnp
from jax import lax
from jax.experimental import pallas as pl
from jax.experimental.pallas import tpu as pltpu
from jax.sharding import PartitionSpec as P

HEAD_DIM = 128
STATE = 64
BLOCK = 256
F32 = jnp.float32
BF16 = jnp.bfloat16
VMEM_LIMIT = 40 << 20


def dot(a, b, dims):
    return lax.dot_general(a, b, (dims, ((), ())), preferred_element_type=F32)


def in_hbm(*arrays):
    return [pltpu.with_memory_space_constraint(a, pltpu.HBM) for a in arrays]


NN = ((1,), (0,))
NT = ((1,), (1,))
TN = ((0,), (0,))


def low_lanes(shape):
    return lax.broadcasted_iota(jnp.int32, shape, len(shape) - 1) < STATE


def log_rows(log):
    high = log.astype(BF16)
    rest = log - high.astype(F32)
    middle = rest.astype(BF16)
    low = (rest - middle.astype(F32)).astype(BF16)
    return high, middle, low


def store_message(ref, sums, logs):
    heads = len(sums)
    for h in range(heads):
        ref[h * STATE : (h + 1) * STATE, :] = sums[h].astype(BF16)
    parts = [log_rows(log) for log in logs]
    rows = [parts[h][k].astype(F32) for k in range(3) for h in range(heads)]
    rows = rows + [jnp.zeros_like(rows[0])] * (16 - 3 * heads)
    ref[heads * STATE :, :] = jnp.concatenate(rows, axis=0).astype(BF16)


def message_sum(ref, h):
    return ref[h * STATE : (h + 1) * STATE, :].astype(F32)


def message_log(ref, heads, h):
    tail = ref[heads * STATE :, :].astype(F32)
    return tail[h : h + 1] + tail[heads + h : heads + h + 1] + tail[2 * heads + h : 2 * heads + h + 1]


def masked_total(terms):
    total = jnp.zeros_like(terms[0][1])
    for condition, value in terms:
        total = total + jnp.where(condition, value, 0.0)
    return total


def combine(kind, place, messages):
    rows, width = messages[0].shape
    heads = (rows - 16) // STATE

    def body(place_ref, *refs):
        got, out_ref = refs[:-1], refs[-1]
        sums, logs = [], []
        for h in range(heads):
            log = [message_log(ref, heads, h) for ref in got]
            if kind == "core":
                first = place_ref[2] == 0
                own = jnp.exp(jnp.where(first, 0.0, log[1]))
                other = jnp.exp(jnp.where(first, log[0], 0.0))
                sums.append(own * message_sum(got[0], h) + other * message_sum(got[1], h))
            else:
                here = [lax.rem(place_ref[1] - s + 4, 4) for s in range(4)]
                total = None
                for s in range(4):
                    ahead = masked_total([(here[t] < here[s], log[t]) for t in range(4) if t != s])
                    term = jnp.exp(ahead) * message_sum(got[s], h)
                    total = term if total is None else total + term
                sums.append(total)
            logs.append(sum(log[1:], log[0]))
        store_message(out_ref, sums, logs)

    return pl.pallas_call(
        body,
        name="combine_" + kind,
        in_specs=[pl.BlockSpec(memory_space=pltpu.SMEM)]
        + [pl.BlockSpec(memory_space=pltpu.VMEM)] * len(messages),
        out_specs=pl.BlockSpec(memory_space=pltpu.VMEM),
        out_shape=jax.ShapeDtypeStruct((rows, width), BF16),
        cost_estimate=pl.CostEstimate(flops=1_000_000, bytes_accessed=500_000, transcendentals=0),
        compiler_params=pltpu.CompilerParams(vmem_limit_bytes=16 << 20),
    )(place, *messages)


def prepare(bc, arow, aline, states):
    tokens, width = bc.shape
    heads = width // HEAD_DIM
    blocks = tokens // BLOCK

    def body(bc_ref, arow_ref, aline_ref, states_ref, sw_ref, dec_ref, sct_ref, wct_ref, spad_ref):
        rows = lax.broadcasted_iota(jnp.int32, (BLOCK, BLOCK), 0)
        cols = lax.broadcasted_iota(jnp.int32, (BLOCK, BLOCK), 1)
        low = low_lanes((BLOCK, HEAD_DIM))
        for h in range(heads):
            lanes = slice(h * HEAD_DIM, (h + 1) * HEAD_DIM)
            gap = aline_ref[:, h : h + 1] - arow_ref[h : h + 1, :]
            dec_ref[0, h] = jnp.where(rows >= cols, jnp.exp(jnp.minimum(gap, 0.0)), 0.0).astype(BF16)
            bc = bc_ref[:, lanes].astype(F32)
            swapped = pltpu.roll(bc, STATE, 1)
            sw_ref[:, lanes] = swapped.astype(BF16)
            c_low = jnp.where(low, swapped, 0.0)
            b_low = jnp.where(low, bc, 0.0)
            scores = dot(b_low.astype(BF16), c_low.astype(BF16), NT)
            back = jnp.where(cols >= rows, jnp.exp(jnp.minimum(-gap, 0.0)), 0.0)
            sct_ref[0, h] = (scores * back).astype(BF16)
            weighted = c_low * jnp.exp(aline_ref[:, h : h + 1])
            wct_ref[0, h] = weighted.T[:STATE, :].astype(BF16)
            state = states_ref[0, h].astype(BF16)
            spad_ref[0, h] = jnp.concatenate([jnp.zeros_like(state), state], axis=0)

    wide = pl.BlockSpec((BLOCK, width), lambda b: (b, 0))

    def block4(*dims):
        return pl.BlockSpec((1, heads) + dims, lambda b: (b, 0, 0, 0))

    return pl.pallas_call(
        body,
        name="prepare",
        grid=(blocks,),
        in_specs=[
            wide,
            pl.BlockSpec((heads, BLOCK), lambda b: (0, b)),
            pl.BlockSpec((BLOCK, heads), lambda b: (b, 0)),
            block4(STATE, HEAD_DIM),
        ],
        out_specs=[
            wide,
            block4(BLOCK, BLOCK),
            block4(BLOCK, BLOCK),
            block4(STATE, BLOCK),
            block4(HEAD_DIM, HEAD_DIM),
        ],
        out_shape=[
            pltpu.HBM((tokens, width), BF16),
            pltpu.HBM((blocks, heads, BLOCK, BLOCK), BF16),
            pltpu.HBM((blocks, heads, BLOCK, BLOCK), BF16),
            pltpu.HBM((blocks, heads, STATE, BLOCK), BF16),
            pltpu.HBM((blocks, heads, HEAD_DIM, HEAD_DIM), BF16),
        ],
        cost_estimate=pl.CostEstimate(flops=4_000_000_000, bytes_accessed=9_000_000, transcendentals=0),
        compiler_params=pltpu.CompilerParams(vmem_limit_bytes=VMEM_LIMIT),
    )(bc, arow, aline, states)


def resident():
    return pl.BlockSpec(memory_space=pltpu.VMEM)


def split_rows(array, count):
    rows, width = array.shape
    part = rows // count

    def body(source_ref, *refs):
        outs, sem = refs[:-1], refs[-1]
        copies = [
            pltpu.make_async_copy(source_ref.at[i * part : (i + 1) * part], out, sem.at[i])
            for i, out in enumerate(outs)
        ]
        for copy in copies:
            copy.start()
        for copy in copies:
            copy.wait()

    return pl.pallas_call(
        body,
        name="split_rows",
        in_specs=[pl.BlockSpec(memory_space=pltpu.HBM)],
        out_specs=[resident()] * count,
        out_shape=[jax.ShapeDtypeStruct((part, width), array.dtype)] * count,
        scratch_shapes=[pltpu.SemaphoreType.DMA((count,))],
        cost_estimate=pl.CostEstimate(flops=0, bytes_accessed=2 * rows * width * 2, transcendentals=0),
        compiler_params=pltpu.CompilerParams(vmem_limit_bytes=16 << 20),
    )(*in_hbm(array))


def close_chunk(first, source, acc, up, down, weight, wct, scale, earlier):
    tokens, width = acc.shape
    heads = width // HEAD_DIM
    feats = up.shape[1]
    last = earlier is not None

    def body(source_ref, scale_ref, acc_ref, up_ref, down_ref, weight_ref, wct_ref, *refs):
        if last:
            earlier_ref, dy_ref, terms_ref, part_ref = refs
        else:
            dy_ref, terms_ref = refs
        weights = weight_ref[:, pl.ds(pl.multiple_of(source_ref[0] * feats, feats), feats)]
        sums = [jnp.zeros((STATE, HEAD_DIM), F32) for _ in range(heads)]
        if last:
            for b in range(2):
                for h in range(heads):
                    sums[h] = sums[h] + scale_ref[b, h] * earlier_ref[b, h]
        for b, piece in enumerate((up_ref, down_ref)):
            rows = slice(b * BLOCK, (b + 1) * BLOCK)
            dy = (acc_ref[rows, :] + dot(piece[...], weights, NT)).astype(BF16)
            dy_ref[rows, :] = dy
            for h in range(heads):
                term = dot(wct_ref[first + b, h], dy[:, h * HEAD_DIM : (h + 1) * HEAD_DIM], NN)
                terms_ref[b, h] = term
                if last:
                    sums[h] = sums[h] + scale_ref[b + first, h] * term
        if last:
            store_message(
                part_ref, sums, [jnp.full((1, HEAD_DIM), scale_ref[4, h], F32) for h in range(heads)]
            )

    smem = pl.BlockSpec(memory_space=pltpu.SMEM)
    out_shape = [
        jax.ShapeDtypeStruct((tokens, width), BF16),
        jax.ShapeDtypeStruct((2, heads, STATE, HEAD_DIM), F32),
    ]
    operands = [source, scale, acc, up, down, weight, wct]
    if last:
        out_shape.append(jax.ShapeDtypeStruct((heads * STATE + 16, HEAD_DIM), BF16))
        operands.append(earlier)
    return pl.pallas_call(
        body,
        name="close_chunk",
        in_specs=[smem, smem] + [resident()] * (len(operands) - 2),
        out_specs=[resident()] * len(out_shape),
        out_shape=out_shape,
        cost_estimate=pl.CostEstimate(flops=600_000_000, bytes_accessed=4_000_000, transcendentals=0),
        compiler_params=pltpu.CompilerParams(vmem_limit_bytes=VMEM_LIMIT),
    )(*operands)


def inside(first, count, dy_first, dy, skip, x, bc, sw, rise, dec, sct, spad):
    width = x.shape[1]
    heads = width // HEAD_DIM

    def body(skip_ref, dy_ref, x_ref, bc_ref, sw_ref, rise_ref, dec_ref, sct_ref, spad_ref, dx_ref, dbc_ref, dlog_ref):
        b = pl.program_id(0)
        here = pl.ds(pl.multiple_of((b + dy_first) * BLOCK, BLOCK), BLOCK)
        there = pl.ds(pl.multiple_of(b * BLOCK, BLOCK), BLOCK)
        rows = lax.broadcasted_iota(jnp.int32, (BLOCK, BLOCK), 0)
        cols = lax.broadcasted_iota(jnp.int32, (BLOCK, BLOCK), 1)
        low = low_lanes((BLOCK, HEAD_DIM))
        for h in range(heads):
            lanes = slice(h * HEAD_DIM, (h + 1) * HEAD_DIM)
            dy_h = dy_ref[here, lanes]
            x_h = x_ref[:, lanes]
            bc_h = bc_ref[:, lanes]
            sw_h = sw_ref[:, lanes]
            zero = jnp.zeros_like(sw_h)
            gaps = dot(dy_h, x_h, NT)
            mixed = (gaps * dec_ref[0, h].astype(F32)).astype(BF16)
            dx_ref[there, lanes] = dot(sct_ref[0, h], dy_h, NN) + skip_ref[0, h] * dy_h.astype(F32)
            grad = dot(mixed, jnp.where(low, zero, sw_h), NN)
            grad = grad + dot(mixed, jnp.where(low, sw_h, zero), TN)
            grad = grad + rise_ref[:, h : h + 1] * dot(dy_h, spad_ref[0, h], NT)
            dbc_ref[there, lanes] = grad
            signed = grad * bc_h.astype(F32)
            moved = jnp.sum(jnp.where(low, -signed, signed), axis=1, keepdims=True)
            dlog_ref[b, h : h + 1, :] = jnp.sum(jnp.where(rows >= cols, moved, 0.0), axis=0, keepdims=True)

    wide = pl.BlockSpec((BLOCK, width), lambda b: (b + first, 0))
    square = pl.BlockSpec((1, heads, BLOCK, BLOCK), lambda b: (b + first, 0, 0, 0))
    x, bc, sw, dec, sct, spad = in_hbm(x, bc, sw, dec, sct, spad)
    return pl.pallas_call(
        body,
        name="inside",
        grid=(count,),
        in_specs=[
            pl.BlockSpec(memory_space=pltpu.SMEM),
            resident(),
            wide,
            wide,
            wide,
            pl.BlockSpec((BLOCK, heads), lambda b: (b + first, 0)),
            square,
            square,
            pl.BlockSpec((1, heads, HEAD_DIM, HEAD_DIM), lambda b: (b + first, 0, 0, 0)),
        ],
        out_specs=[resident()] * 3,
        out_shape=[
            jax.ShapeDtypeStruct((count * BLOCK, width), F32),
            jax.ShapeDtypeStruct((count * BLOCK, width), F32),
            jax.ShapeDtypeStruct((count, heads, BLOCK), F32),
        ],
        cost_estimate=pl.CostEstimate(
            flops=1_000_000_000 * count, bytes_accessed=3_500_000 * count, transcendentals=0
        ),
        compiler_params=pltpu.CompilerParams(vmem_limit_bytes=VMEM_LIMIT),
    )(skip, dy, x, bc, sw, rise, dec, sct, spad)


def finish(place, a_last, received, x, bc, fall, terms, states, grads):
    tokens, width = x.shape
    heads = width // HEAD_DIM
    blocks = tokens // BLOCK
    count = len(received)
    starts = [first for first, *_ in grads] + [blocks]
    flat = [array for _, *arrays in grads for array in arrays]

    def body(place_ref, last_ref, *refs):
        got = refs[:count]
        x_ref, bc_ref, fall_ref, terms0_ref, terms1_ref, states_ref = refs[count : count + 6]
        grad_refs = refs[count + 6 : -4]
        out_ref, outbc_ref, outlog_ref, carry_ref = refs[-4:]
        step = pl.program_id(0)
        b = blocks - 1 - step

        @pl.when(step == 0)
        def _():
            own, other, ys, xs = got[0], got[1], got[2:6], got[6:10]
            first = place_ref[2] == 0
            at_y = [lax.rem(place_ref[1] - s + 4, 4) for s in range(4)]
            at_x = [lax.rem(place_ref[0] - s + 4, 4) for s in range(4)]
            for h in range(heads):
                y_logs = [message_log(ref, heads, h) for ref in ys]
                x_logs = [message_log(ref, heads, h) for ref in xs]
                after_core = jnp.where(first, message_log(other, heads, h), 0.0)
                after_y = after_core + masked_total([(at_y[t] > at_y[0], y_logs[t]) for t in (1, 2, 3)])
                total = jnp.where(first, message_sum(other, h), 0.0)
                for places, logs, items, after in ((at_y, y_logs, ys, after_core), (at_x, x_logs, xs, after_y)):
                    for s in (1, 2, 3):
                        between = masked_total(
                            [
                                ((places[t] > places[0]) & (places[t] < places[s]), logs[t])
                                for t in (1, 2, 3)
                                if t != s
                            ]
                        )
                        factor = jnp.where(places[s] > places[0], jnp.exp(after + between), 0.0)
                        total = total + factor * message_sum(items[s], h)
                carry_ref[h] = total

        rows = lax.broadcasted_iota(jnp.int32, (BLOCK, BLOCK), 0)
        cols = lax.broadcasted_iota(jnp.int32, (BLOCK, BLOCK), 1)

        def run(first, dx_ref, dbc_ref, dlog_ref):
            here = pl.ds(pl.multiple_of((b - first) * BLOCK, BLOCK), BLOCK)
            terms_ref = terms0_ref if first < 2 else terms1_ref
            for h in range(heads):
                lanes = slice(h * HEAD_DIM, (h + 1) * HEAD_DIM)
                carry = carry_ref[h]
                carry16 = carry.astype(BF16)
                tail = fall_ref[:, h : h + 1]
                bc_h = bc_ref[:, lanes].astype(F32)
                weighted = (bc_h * tail).astype(BF16)[:, :STATE]
                out_ref[:, lanes] = (dx_ref[here, lanes] + dot(weighted, carry16, NN)).astype(BF16)
                padded = jnp.concatenate([carry16, jnp.zeros_like(carry16)], axis=0)
                extra = tail * dot(x_ref[:, lanes], padded, NT)
                outbc_ref[:, lanes] = dbc_ref[here, lanes] + extra
                moved = jnp.sum(extra * bc_h, axis=1, keepdims=True)
                ends = jnp.exp(jnp.full((1, HEAD_DIM), last_ref[b, h], F32))
                whole = jnp.sum(jnp.sum(states_ref[0, h] * carry, axis=0, keepdims=True) * ends)
                outlog_ref[h : h + 1, :] = (
                    dlog_ref[b - first, h : h + 1, :]
                    + jnp.sum(jnp.where(rows < cols, moved, 0.0), axis=0, keepdims=True)
                    + whole
                )
                carry_ref[h] = ends * carry + terms_ref[b % 2, h]

        for k in range(len(grads)):

            @pl.when((b >= starts[k]) & (b < starts[k + 1]))
            def _(k=k):
                run(starts[k], *grad_refs[3 * k : 3 * k + 3])

    x, bc, states = in_hbm(x, bc, states)
    wide = pl.BlockSpec((BLOCK, width), lambda i: (blocks - 1 - i, 0))
    smem = pl.BlockSpec(memory_space=pltpu.SMEM)
    return pl.pallas_call(
        body,
        name="finish",
        grid=(blocks,),
        in_specs=[smem, smem]
        + [resident()] * count
        + [
            wide,
            wide,
            pl.BlockSpec((BLOCK, heads), lambda i: (blocks - 1 - i, 0)),
            resident(),
            resident(),
            pl.BlockSpec((1, heads, STATE, HEAD_DIM), lambda i: (blocks - 1 - i, 0, 0, 0)),
        ]
        + [resident()] * len(flat),
        out_specs=[wide, wide, pl.BlockSpec((heads, BLOCK), lambda i: (0, blocks - 1 - i))],
        out_shape=[
            jax.ShapeDtypeStruct((tokens, width), BF16),
            jax.ShapeDtypeStruct((tokens, width), F32),
            jax.ShapeDtypeStruct((heads, tokens), F32),
        ],
        scratch_shapes=[pltpu.VMEM((heads, STATE, HEAD_DIM), F32)],
        cost_estimate=pl.CostEstimate(flops=600_000_000, bytes_accessed=11_000_000, transcendentals=0),
        compiler_params=pltpu.CompilerParams(vmem_limit_bytes=VMEM_LIMIT),
    )(place, a_last, *received, x, bc, fall, terms[0], terms[1], states, *flat)


def shift(count, by):
    return [(i, (i + by) % count) for i in range(count)]


def per_device(upstream, out_weight, inner_act, head_bc, log_decay, states, skip):
    tokens, width = inner_act.shape
    heads = log_decay.shape[0]
    blocks = tokens // BLOCK
    tp = lax.axis_size("tp")
    me = lax.axis_index("tp")
    ctx = lax.axis_index("ctx")
    feats = upstream.shape[1]
    px, py, pc = ctx // 8, (ctx // 2) % 4, ctx % 2

    places = [(x, y, c) for x in range(4) for y in range(4) for c in range(2)]

    def perm(dx, dy, dc):
        return [(x * 8 + y * 2 + c, ((x + dx) % 4) * 8 + ((y + dy) % 4) * 2 + (c ^ dc)) for x, y, c in places]

    def from_core(a):
        return lax.ppermute(a, "ctx", perm(0, 0, 1))

    def from_y(a):
        return [lax.ppermute(a, "ctx", perm(0, s, 0)) for s in (1, 2, 3)]

    def from_x(a):
        return [lax.ppermute(a, "ctx", perm(s, 0, 0)) for s in (1, 2, 3)]

    def weight_of(source):
        return lax.dynamic_slice_in_dim(out_weight, (source % tp) * feats, feats, 1)

    half = tokens // 2
    accs, lasts, firsts = [], [], []
    owns = split_rows(upstream, 2)
    for c in range(2):
        own = owns[c]
        right = left = own
        acc = dot(own, weight_of(me), NT)
        for k in range(1, tp // 2):
            right = lax.ppermute(right, "tp", shift(tp, 1))
            left = lax.ppermute(left, "tp", shift(tp, -1))
            if k == 1:
                firsts.append(right)
            acc = acc + dot(right, weight_of(me - k + tp), NT) + dot(left, weight_of(me + k), NT)
        up = lax.ppermute(right[:BLOCK], "tp", shift(tp, 1))
        down = lax.ppermute(left[BLOCK:], "tp", shift(tp, -1))
        accs.append(acc)
        lasts.append((up, down))

    triangle = (jnp.arange(BLOCK)[:, None] <= jnp.arange(BLOCK)[None, :]).astype(F32)
    cum = jnp.dot(log_decay.reshape(heads * blocks, BLOCK), triangle, precision=lax.Precision.HIGHEST)
    cum = cum.reshape(heads, blocks, BLOCK)
    last = cum[:, :, -1].T
    arow = cum.reshape(heads, tokens)
    aline = arow.T
    bc_then, _ = lax.optimization_barrier((head_bc, firsts[0]))
    sw, dec, sct, wct, spad = prepare(bc_then, arow, aline, states)
    upto = jnp.cumsum(last, axis=0)
    scale = jnp.concatenate([jnp.exp(upto - last), upto[blocks - 1 :]])
    place = jnp.stack([px, py, pc]).astype(jnp.int32)

    skips = skip[None]
    rise = jnp.exp(aline)
    fall = jnp.exp((cum[:, :, -1:] - cum).reshape(heads, tokens).T)

    def within(first, count, dy_first, dy):
        grads = inside(first, count, dy_first, dy, skips, inner_act, head_bc, sw, rise, dec, sct, spad)
        return (first, *grads)

    source = ((me + tp // 2) % tp).astype(jnp.int32)[None]
    dy0, terms0 = close_chunk(0, source, accs[0], *lasts[0], out_weight, wct, scale, None)
    grads0 = within(0, 1, 0, dy0)
    terms0, last_grad, fall = lax.optimization_barrier((terms0, grads0[3], fall))
    grads0 = grads0[:3] + (last_grad,)
    dy1, terms1, part = close_chunk(2, source, accs[1], *lasts[1], out_weight, wct, scale, terms0)
    other = from_core(part)
    chip = combine("core", place, [part, other])
    ys = [chip] + from_y(chip)
    dy0, ys[0] = lax.optimization_barrier((dy0, ys[0]))
    grads1 = within(1, 1, 1, dy0)
    row = combine("row", place, ys)
    xs = [row] + from_x(row)
    dy1, xs[0] = lax.optimization_barrier((dy1, xs[0]))
    grads2 = within(2, 2, 0, dy1)
    return finish(
        place, last, [part, other] + ys + xs, inner_act, head_bc, fall, (terms0, terms1), states,
        [grads0, grads1, grads2],
    )


def solution(mesh):
    return jax.shard_map(
        per_device,
        mesh=mesh,
        in_specs=(
            P("ctx", "tp"),
            P("tp", None),
            P("ctx", "tp"),
            P("ctx", "tp"),
            P("tp", "ctx"),
            P("ctx", "tp", None, None),
            P("tp"),
        ),
        out_specs=(P("ctx", "tp"), P("ctx", "tp"), P("tp", "ctx")),
        check_vma=False,
    )
```

```python
import jax
import jax.numpy as jnp
from jax import lax
from jax.experimental import pallas as pl
from jax.experimental.pallas import tpu as pltpu
from jax.sharding import PartitionSpec as P

HEAD_DIM = 128
STATE = 64
BLOCK = 256
F32 = jnp.float32
BF16 = jnp.bfloat16
VMEM_LIMIT = 40 << 20


def dot(a, b, dims):
    return lax.dot_general(a, b, (dims, ((), ())), preferred_element_type=F32)


def in_hbm(*arrays):
    return [pltpu.with_memory_space_constraint(a, pltpu.HBM) for a in arrays]


NN = ((1,), (0,))
NT = ((1,), (1,))
TN = ((0,), (0,))


def low_lanes(shape):
    return lax.broadcasted_iota(jnp.int32, shape, len(shape) - 1) < STATE


def log_rows(log):
    high = log.astype(BF16)
    rest = log - high.astype(F32)
    middle = rest.astype(BF16)
    low = (rest - middle.astype(F32)).astype(BF16)
    return high, middle, low


def store_message(ref, sums, logs):
    heads = len(sums)
    for h in range(heads):
        ref[h * STATE : (h + 1) * STATE, :] = sums[h].astype(BF16)
    parts = [log_rows(log) for log in logs]
    rows = [parts[h][k].astype(F32) for k in range(3) for h in range(heads)]
    rows = rows + [jnp.zeros_like(rows[0])] * (16 - 3 * heads)
    ref[heads * STATE :, :] = jnp.concatenate(rows, axis=0).astype(BF16)


def message_sum(ref, h):
    return ref[h * STATE : (h + 1) * STATE, :].astype(F32)


def message_log(ref, heads, h):
    tail = ref[heads * STATE :, :].astype(F32)
    return tail[h : h + 1] + tail[heads + h : heads + h + 1] + tail[2 * heads + h : 2 * heads + h + 1]


def masked_total(terms):
    total = jnp.zeros_like(terms[0][1])
    for condition, value in terms:
        total = total + jnp.where(condition, value, 0.0)
    return total


def combine(kind, place, messages):
    rows, width = messages[0].shape
    heads = (rows - 16) // STATE

    def body(place_ref, *refs):
        got, out_ref = refs[:-1], refs[-1]
        sums, logs = [], []
        for h in range(heads):
            log = [message_log(ref, heads, h) for ref in got]
            if kind == "core":
                first = place_ref[2] == 0
                own = jnp.exp(jnp.where(first, 0.0, log[1]))
                other = jnp.exp(jnp.where(first, log[0], 0.0))
                sums.append(own * message_sum(got[0], h) + other * message_sum(got[1], h))
            else:
                here = [lax.rem(place_ref[1] - s + 4, 4) for s in range(4)]
                total = None
                for s in range(4):
                    ahead = masked_total([(here[t] < here[s], log[t]) for t in range(4) if t != s])
                    term = jnp.exp(ahead) * message_sum(got[s], h)
                    total = term if total is None else total + term
                sums.append(total)
            logs.append(sum(log[1:], log[0]))
        store_message(out_ref, sums, logs)

    return pl.pallas_call(
        body,
        name="combine_" + kind,
        in_specs=[pl.BlockSpec(memory_space=pltpu.SMEM)]
        + [pl.BlockSpec(memory_space=pltpu.VMEM)] * len(messages),
        out_specs=pl.BlockSpec(memory_space=pltpu.VMEM),
        out_shape=jax.ShapeDtypeStruct((rows, width), BF16),
        cost_estimate=pl.CostEstimate(flops=1_000_000, bytes_accessed=500_000, transcendentals=0),
        compiler_params=pltpu.CompilerParams(vmem_limit_bytes=16 << 20),
    )(place, *messages)


def prepare(bc, arow, aline, states):
    tokens, width = bc.shape
    heads = width // HEAD_DIM
    blocks = tokens // BLOCK

    def body(bc_ref, arow_ref, aline_ref, states_ref, sw_ref, dec_ref, sct_ref, wct_ref, spad_ref):
        rows = lax.broadcasted_iota(jnp.int32, (BLOCK, BLOCK), 0)
        cols = lax.broadcasted_iota(jnp.int32, (BLOCK, BLOCK), 1)
        low = low_lanes((BLOCK, HEAD_DIM))
        for h in range(heads):
            lanes = slice(h * HEAD_DIM, (h + 1) * HEAD_DIM)
            gap = aline_ref[:, h : h + 1] - arow_ref[h : h + 1, :]
            dec_ref[0, h] = jnp.where(rows >= cols, jnp.exp(jnp.minimum(gap, 0.0)), 0.0).astype(BF16)
            bc = bc_ref[:, lanes].astype(F32)
            swapped = pltpu.roll(bc, STATE, 1)
            sw_ref[:, lanes] = swapped.astype(BF16)
            c_low = jnp.where(low, swapped, 0.0)
            b_low = jnp.where(low, bc, 0.0)
            scores = dot(b_low.astype(BF16), c_low.astype(BF16), NT)
            back = jnp.where(cols >= rows, jnp.exp(jnp.minimum(-gap, 0.0)), 0.0)
            sct_ref[0, h] = (scores * back).astype(BF16)
            weighted = c_low * jnp.exp(aline_ref[:, h : h + 1])
            wct_ref[0, h] = weighted.T[:STATE, :].astype(BF16)
            state = states_ref[0, h].astype(BF16)
            spad_ref[0, h] = jnp.concatenate([jnp.zeros_like(state), state], axis=0)

    wide = pl.BlockSpec((BLOCK, width), lambda b: (b, 0))

    def block4(*dims):
        return pl.BlockSpec((1, heads) + dims, lambda b: (b, 0, 0, 0))

    return pl.pallas_call(
        body,
        name="prepare",
        grid=(blocks,),
        in_specs=[
            wide,
            pl.BlockSpec((heads, BLOCK), lambda b: (0, b)),
            pl.BlockSpec((BLOCK, heads), lambda b: (b, 0)),
            block4(STATE, HEAD_DIM),
        ],
        out_specs=[
            wide,
            block4(BLOCK, BLOCK),
            block4(BLOCK, BLOCK),
            block4(STATE, BLOCK),
            block4(HEAD_DIM, HEAD_DIM),
        ],
        out_shape=[
            pltpu.HBM((tokens, width), BF16),
            pltpu.HBM((blocks, heads, BLOCK, BLOCK), BF16),
            pltpu.HBM((blocks, heads, BLOCK, BLOCK), BF16),
            pltpu.HBM((blocks, heads, STATE, BLOCK), BF16),
            pltpu.HBM((blocks, heads, HEAD_DIM, HEAD_DIM), BF16),
        ],
        cost_estimate=pl.CostEstimate(flops=4_000_000_000, bytes_accessed=9_000_000, transcendentals=0),
        compiler_params=pltpu.CompilerParams(vmem_limit_bytes=VMEM_LIMIT),
    )(bc, arow, aline, states)


def resident():
    return pl.BlockSpec(memory_space=pltpu.VMEM)


def split_rows(array, count):
    rows, width = array.shape
    part = rows // count

    def body(source_ref, *refs):
        outs, sem = refs[:-1], refs[-1]
        copies = [
            pltpu.make_async_copy(source_ref.at[i * part : (i + 1) * part], out, sem.at[i])
            for i, out in enumerate(outs)
        ]
        for copy in copies:
            copy.start()
        for copy in copies:
            copy.wait()

    return pl.pallas_call(
        body,
        name="split_rows",
        in_specs=[pl.BlockSpec(memory_space=pltpu.HBM)],
        out_specs=[resident()] * count,
        out_shape=[jax.ShapeDtypeStruct((part, width), array.dtype)] * count,
        scratch_shapes=[pltpu.SemaphoreType.DMA((count,))],
        cost_estimate=pl.CostEstimate(flops=0, bytes_accessed=2 * rows * width * 2, transcendentals=0),
        compiler_params=pltpu.CompilerParams(vmem_limit_bytes=16 << 20),
    )(*in_hbm(array))


def close_chunk(first, source, acc, up, down, weight, wct, scale, earlier):
    tokens, width = acc.shape
    heads = width // HEAD_DIM
    feats = up.shape[1]
    last = earlier is not None

    def body(source_ref, scale_ref, acc_ref, up_ref, down_ref, weight_ref, wct_ref, *refs):
        if last:
            earlier_ref, dy_ref, terms_ref, part_ref = refs
        else:
            dy_ref, terms_ref = refs
        weights = weight_ref[:, pl.ds(pl.multiple_of(source_ref[0] * feats, feats), feats)]
        sums = [jnp.zeros((STATE, HEAD_DIM), F32) for _ in range(heads)]
        if last:
            for b in range(2):
                for h in range(heads):
                    sums[h] = sums[h] + scale_ref[b, h] * earlier_ref[b, h]
        for b, piece in enumerate((up_ref, down_ref)):
            rows = slice(b * BLOCK, (b + 1) * BLOCK)
            dy = (acc_ref[rows, :] + dot(piece[...], weights, NT)).astype(BF16)
            dy_ref[rows, :] = dy
            for h in range(heads):
                term = dot(wct_ref[first + b, h], dy[:, h * HEAD_DIM : (h + 1) * HEAD_DIM], NN)
                terms_ref[b, h] = term
                if last:
                    sums[h] = sums[h] + scale_ref[b + first, h] * term
        if last:
            store_message(
                part_ref, sums, [jnp.full((1, HEAD_DIM), scale_ref[4, h], F32) for h in range(heads)]
            )

    smem = pl.BlockSpec(memory_space=pltpu.SMEM)
    out_shape = [
        jax.ShapeDtypeStruct((tokens, width), BF16),
        jax.ShapeDtypeStruct((2, heads, STATE, HEAD_DIM), F32),
    ]
    operands = [source, scale, acc, up, down, weight, wct]
    if last:
        out_shape.append(jax.ShapeDtypeStruct((heads * STATE + 16, HEAD_DIM), BF16))
        operands.append(earlier)
    return pl.pallas_call(
        body,
        name="close_chunk",
        in_specs=[smem, smem] + [resident()] * (len(operands) - 2),
        out_specs=[resident()] * len(out_shape),
        out_shape=out_shape,
        cost_estimate=pl.CostEstimate(flops=600_000_000, bytes_accessed=4_000_000, transcendentals=0),
        compiler_params=pltpu.CompilerParams(vmem_limit_bytes=VMEM_LIMIT),
    )(*operands)


def inside(first, count, dy_first, dy, skip, x, bc, sw, rise, dec, sct, spad):
    width = x.shape[1]
    heads = width // HEAD_DIM

    def body(skip_ref, dy_ref, x_ref, bc_ref, sw_ref, rise_ref, dec_ref, sct_ref, spad_ref, dx_ref, dbc_ref, dlog_ref):
        b = pl.program_id(0)
        here = pl.ds(pl.multiple_of((b + dy_first) * BLOCK, BLOCK), BLOCK)
        there = pl.ds(pl.multiple_of(b * BLOCK, BLOCK), BLOCK)
        rows = lax.broadcasted_iota(jnp.int32, (BLOCK, BLOCK), 0)
        cols = lax.broadcasted_iota(jnp.int32, (BLOCK, BLOCK), 1)
        low = low_lanes((BLOCK, HEAD_DIM))
        for h in range(heads):
            lanes = slice(h * HEAD_DIM, (h + 1) * HEAD_DIM)
            dy_h = dy_ref[here, lanes]
            x_h = x_ref[:, lanes]
            bc_h = bc_ref[:, lanes]
            sw_h = sw_ref[:, lanes]
            zero = jnp.zeros_like(sw_h)
            gaps = dot(dy_h, x_h, NT)
            mixed = (gaps * dec_ref[0, h].astype(F32)).astype(BF16)
            dx_ref[there, lanes] = dot(sct_ref[0, h], dy_h, NN) + skip_ref[0, h] * dy_h.astype(F32)
            grad = dot(mixed, jnp.where(low, zero, sw_h), NN)
            grad = grad + dot(mixed, jnp.where(low, sw_h, zero), TN)
            grad = grad + rise_ref[:, h : h + 1] * dot(dy_h, spad_ref[0, h], NT)
            dbc_ref[there, lanes] = grad
            signed = grad * bc_h.astype(F32)
            moved = jnp.sum(jnp.where(low, -signed, signed), axis=1, keepdims=True)
            dlog_ref[b, h : h + 1, :] = jnp.sum(jnp.where(rows >= cols, moved, 0.0), axis=0, keepdims=True)

    wide = pl.BlockSpec((BLOCK, width), lambda b: (b + first, 0))
    square = pl.BlockSpec((1, heads, BLOCK, BLOCK), lambda b: (b + first, 0, 0, 0))
    x, bc, sw, dec, sct, spad = in_hbm(x, bc, sw, dec, sct, spad)
    return pl.pallas_call(
        body,
        name="inside",
        grid=(count,),
        in_specs=[
            pl.BlockSpec(memory_space=pltpu.SMEM),
            resident(),
            wide,
            wide,
            wide,
            pl.BlockSpec((BLOCK, heads), lambda b: (b + first, 0)),
            square,
            square,
            pl.BlockSpec((1, heads, HEAD_DIM, HEAD_DIM), lambda b: (b + first, 0, 0, 0)),
        ],
        out_specs=[resident()] * 3,
        out_shape=[
            jax.ShapeDtypeStruct((count * BLOCK, width), F32),
            jax.ShapeDtypeStruct((count * BLOCK, width), F32),
            jax.ShapeDtypeStruct((count, heads, BLOCK), F32),
        ],
        cost_estimate=pl.CostEstimate(
            flops=1_000_000_000 * count, bytes_accessed=3_500_000 * count, transcendentals=0
        ),
        compiler_params=pltpu.CompilerParams(vmem_limit_bytes=VMEM_LIMIT),
    )(skip, dy, x, bc, sw, rise, dec, sct, spad)


def finish(place, a_last, received, x, bc, fall, terms, states, grads):
    tokens, width = x.shape
    heads = width // HEAD_DIM
    blocks = tokens // BLOCK
    count = len(received)
    starts = [first for first, *_ in grads] + [blocks]
    flat = [array for _, *arrays in grads for array in arrays]

    def body(place_ref, last_ref, *refs):
        got = refs[:count]
        x_ref, bc_ref, fall_ref, terms0_ref, terms1_ref, states_ref = refs[count : count + 6]
        grad_refs = refs[count + 6 : -4]
        out_ref, outbc_ref, outlog_ref, carry_ref = refs[-4:]
        step = pl.program_id(0)
        b = blocks - 1 - step

        @pl.when(step == 0)
        def _():
            own, other, ys, xs = got[0], got[1], got[2:6], got[6:10]
            first = place_ref[2] == 0
            at_y = [lax.rem(place_ref[1] - s + 4, 4) for s in range(4)]
            at_x = [lax.rem(place_ref[0] - s + 4, 4) for s in range(4)]
            for h in range(heads):
                y_logs = [message_log(ref, heads, h) for ref in ys]
                x_logs = [message_log(ref, heads, h) for ref in xs]
                after_core = jnp.where(first, message_log(other, heads, h), 0.0)
                after_y = after_core + masked_total([(at_y[t] > at_y[0], y_logs[t]) for t in (1, 2, 3)])
                total = jnp.where(first, message_sum(other, h), 0.0)
                for places, logs, items, after in ((at_y, y_logs, ys, after_core), (at_x, x_logs, xs, after_y)):
                    for s in (1, 2, 3):
                        between = masked_total(
                            [
                                ((places[t] > places[0]) & (places[t] < places[s]), logs[t])
                                for t in (1, 2, 3)
                                if t != s
                            ]
                        )
                        factor = jnp.where(places[s] > places[0], jnp.exp(after + between), 0.0)
                        total = total + factor * message_sum(items[s], h)
                carry_ref[h] = total

        rows = lax.broadcasted_iota(jnp.int32, (BLOCK, BLOCK), 0)
        cols = lax.broadcasted_iota(jnp.int32, (BLOCK, BLOCK), 1)

        def run(first, dx_ref, dbc_ref, dlog_ref):
            here = pl.ds(pl.multiple_of((b - first) * BLOCK, BLOCK), BLOCK)
            terms_ref = terms0_ref if first < 2 else terms1_ref
            for h in range(heads):
                lanes = slice(h * HEAD_DIM, (h + 1) * HEAD_DIM)
                carry = carry_ref[h]
                carry16 = carry.astype(BF16)
                tail = fall_ref[:, h : h + 1]
                bc_h = bc_ref[:, lanes].astype(F32)
                fallen = bc_h * tail
                weighted = fallen.astype(BF16)[:, :STATE]
                out_ref[:, lanes] = (dx_ref[here, lanes] + dot(weighted, carry16, NN)).astype(BF16)
                padded = jnp.concatenate([carry16, jnp.zeros_like(carry16)], axis=0)
                reached = dot(x_ref[:, lanes], padded, NT)
                extra = tail * reached
                outbc_ref[:, lanes] = dbc_ref[here, lanes] + extra
                moved = jnp.sum(reached * fallen, axis=1, keepdims=True)
                ends = jnp.exp(jnp.full((1, HEAD_DIM), last_ref[b, h], F32))
                whole = jnp.sum(jnp.sum(states_ref[0, h] * carry, axis=0, keepdims=True) * ends)
                outlog_ref[h : h + 1, :] = (
                    dlog_ref[b - first, h : h + 1, :]
                    + jnp.sum(jnp.where(rows < cols, moved, 0.0), axis=0, keepdims=True)
                    + whole
                )
                carry_ref[h] = ends * carry + terms_ref[b % 2, h]

        for k in range(len(grads)):

            @pl.when((b >= starts[k]) & (b < starts[k + 1]))
            def _(k=k):
                run(starts[k], *grad_refs[3 * k : 3 * k + 3])

    x, bc, states = in_hbm(x, bc, states)
    wide = pl.BlockSpec((BLOCK, width), lambda i: (blocks - 1 - i, 0))
    smem = pl.BlockSpec(memory_space=pltpu.SMEM)
    return pl.pallas_call(
        body,
        name="finish",
        grid=(blocks,),
        in_specs=[smem, smem]
        + [resident()] * count
        + [
            wide,
            wide,
            pl.BlockSpec((BLOCK, heads), lambda i: (blocks - 1 - i, 0)),
            resident(),
            resident(),
            pl.BlockSpec((1, heads, STATE, HEAD_DIM), lambda i: (blocks - 1 - i, 0, 0, 0)),
        ]
        + [resident()] * len(flat),
        out_specs=[wide, wide, pl.BlockSpec((heads, BLOCK), lambda i: (0, blocks - 1 - i))],
        out_shape=[
            jax.ShapeDtypeStruct((tokens, width), BF16),
            jax.ShapeDtypeStruct((tokens, width), F32),
            jax.ShapeDtypeStruct((heads, tokens), F32),
        ],
        scratch_shapes=[pltpu.VMEM((heads, STATE, HEAD_DIM), F32)],
        cost_estimate=pl.CostEstimate(flops=600_000_000, bytes_accessed=11_000_000, transcendentals=0),
        compiler_params=pltpu.CompilerParams(vmem_limit_bytes=VMEM_LIMIT),
    )(place, a_last, *received, x, bc, fall, terms[0], terms[1], states, *flat)


def shift(count, by):
    return [(i, (i + by) % count) for i in range(count)]


def per_device(upstream, out_weight, inner_act, head_bc, log_decay, states, skip):
    tokens, width = inner_act.shape
    heads = log_decay.shape[0]
    blocks = tokens // BLOCK
    tp = lax.axis_size("tp")
    me = lax.axis_index("tp")
    ctx = lax.axis_index("ctx")
    feats = upstream.shape[1]
    px, py, pc = ctx // 8, (ctx // 2) % 4, ctx % 2

    places = [(x, y, c) for x in range(4) for y in range(4) for c in range(2)]

    def perm(dx, dy, dc):
        return [(x * 8 + y * 2 + c, ((x + dx) % 4) * 8 + ((y + dy) % 4) * 2 + (c ^ dc)) for x, y, c in places]

    def from_core(a):
        return lax.ppermute(a, "ctx", perm(0, 0, 1))

    def from_y(a):
        return [lax.ppermute(a, "ctx", perm(0, s, 0)) for s in (1, 2, 3)]

    def from_x(a):
        return [lax.ppermute(a, "ctx", perm(s, 0, 0)) for s in (1, 2, 3)]

    def weight_of(source):
        return lax.dynamic_slice_in_dim(out_weight, (source % tp) * feats, feats, 1)

    half = tokens // 2
    accs, lasts, firsts = [], [], []
    owns = split_rows(upstream, 2)
    for c in range(2):
        own = owns[c]
        right = left = own
        acc = dot(own, weight_of(me), NT)
        for k in range(1, tp // 2):
            right = lax.ppermute(right, "tp", shift(tp, 1))
            left = lax.ppermute(left, "tp", shift(tp, -1))
            if k == 1:
                firsts.append(right)
            acc = acc + dot(right, weight_of(me - k + tp), NT) + dot(left, weight_of(me + k), NT)
        up = lax.ppermute(right[:BLOCK], "tp", shift(tp, 1))
        down = lax.ppermute(left[BLOCK:], "tp", shift(tp, -1))
        accs.append(acc)
        lasts.append((up, down))

    triangle = (jnp.arange(BLOCK)[:, None] <= jnp.arange(BLOCK)[None, :]).astype(F32)
    cum = jnp.dot(log_decay.reshape(heads * blocks, BLOCK), triangle, precision=lax.Precision.HIGHEST)
    cum = cum.reshape(heads, blocks, BLOCK)
    last = cum[:, :, -1].T
    arow = cum.reshape(heads, tokens)
    aline = arow.T
    bc_then, _ = lax.optimization_barrier((head_bc, firsts[0]))
    sw, dec, sct, wct, spad = prepare(bc_then, arow, aline, states)
    upto = jnp.cumsum(last, axis=0)
    scale = jnp.concatenate([jnp.exp(upto - last), upto[blocks - 1 :]])
    place = jnp.stack([px, py, pc]).astype(jnp.int32)

    skips = skip[None]
    rise = jnp.exp(aline)
    fall = jnp.exp((cum[:, :, -1:] - cum).reshape(heads, tokens).T)

    def within(first, count, dy_first, dy):
        grads = inside(first, count, dy_first, dy, skips, inner_act, head_bc, sw, rise, dec, sct, spad)
        return (first, *grads)

    source = ((me + tp // 2) % tp).astype(jnp.int32)[None]
    dy0, terms0 = close_chunk(0, source, accs[0], *lasts[0], out_weight, wct, scale, None)
    grads0 = within(0, 1, 0, dy0)
    terms0, last_grad, fall = lax.optimization_barrier((terms0, grads0[3], fall))
    grads0 = grads0[:3] + (last_grad,)
    dy1, terms1, part = close_chunk(2, source, accs[1], *lasts[1], out_weight, wct, scale, terms0)
    other = from_core(part)
    chip = combine("core", place, [part, other])
    ys = [chip] + from_y(chip)
    dy0, ys[0] = lax.optimization_barrier((dy0, ys[0]))
    grads1 = within(1, 1, 1, dy0)
    row = combine("row", place, ys)
    xs = [row] + from_x(row)
    dy1, xs[0] = lax.optimization_barrier((dy1, xs[0]))
    grads2 = within(2, 2, 0, dy1)
    return finish(
        place, last, [part, other] + ys + xs, inner_act, head_bc, fall, (terms0, terms1), states,
        [grads0, grads1, grads2],
    )


def solution(mesh):
    return jax.shard_map(
        per_device,
        mesh=mesh,
        in_specs=(
            P("ctx", "tp"),
            P("tp", None),
            P("ctx", "tp"),
            P("ctx", "tp"),
            P("tp", "ctx"),
            P("ctx", "tp", None, None),
            P("tp"),
        ),
        out_specs=(P("ctx", "tp"), P("ctx", "tp"), P("tp", "ctx")),
        check_vma=False,
    )
```
